128 devices in a mesh: req: 8 (over x, y_hi), mdl: 16 (over z, y_lo, core).
Axes of the slice: x: 4, y: 4 (y_hi: 2, y_lo: 2; y = y_hi * 2 + y_lo), z: 4, core: 2. Of those that a mesh axis runs over, the one named last changes fastest.
Arguments:
- tokens: bfloat16 [16384, 1536], P(('req', 'mdl')), may hold values from -3 to 3
- attention_gain: bfloat16 [1536], replicated, may hold values from 0.099609375 to 1.8984375
- feed_gain: bfloat16 [1536], replicated, may hold values from 0.099609375 to 1.8984375
- w_query: bfloat16 [1536, 1536], P('req', 'mdl'), may hold values from -0.4375 to 0.4375
- w_key: bfloat16 [1536, 768], P('req', 'mdl'), may hold values from -0.15625 to 0.15625
- w_value: bfloat16 [1536, 768], P('req', 'mdl'), may hold values from -0.15625 to 0.15625
- w_out: bfloat16 [1536, 1536], P('mdl', 'req'), may hold values from -0.15625 to 0.15625
- w_gate: bfloat16 [1536, 4096], P('req', 'mdl'), may hold values from -0.15625 to 0.15625
- w_up: bfloat16 [1536, 4096], P('req', 'mdl'), may hold values from -0.15625 to 0.15625
- w_down: bfloat16 [4096, 1536], P('mdl', 'req'), may hold values from -0.09375 to 0.09375
- prefix_cache: bfloat16 [2, 8, 4096, 768], P(None, 'req', None, 'mdl'), may hold values from -400 to 400
- lengths: int32 [32], replicated, may hold values from 0 to 512, as said below
- member: int32 [32], replicated, may hold values from 0 to 7
- owners: int32 [8], replicated, may hold values from 0 to 7, as said below
Outputs:
- hidden: bfloat16 [16384, 1536], P(('req', 'mdl'))
- suffix_cache: bfloat16 [2, 16384, 768], P(None, 'req', 'mdl')
The draws below stay inside these ranges and needn't reach their ends.
Inputs may be any that keep to these rules, and one draw needn't show every extreme that they name: `lengths`: some request has 512 live tokens in every draw. Request r reads the prefix of group member[r]. Each slot holds exactly one group: slot owners[g] of prefix_cache holds group g's prefix, whose keys carry rotary encoding at positions 0 to 4095.
All inputs are finite; a program needn't handle non-finite values.
Results may differ from the reference program's by a relative error of at most 0.025.
Values may be sent and summed in bfloat16 or wider, within the bound.
A program may use at most 128 MiB of HBM per device.

```python
import math
import jax
import jax.numpy as jnp
import numpy as np
from jax import lax

D = 1536
HEADS = 16
KV_HEADS = 8
HD = 96
FF = 4096
PLEN = 4096
SUF = 512
QW = 1536
KVW = 768
GROUPS = 8
REQS = 32
TOKENS = 16384
N_MDL = 16


def draw_prefix_cache(key, part):
    first_key = jax.random.fold_in(jax.random.fold_in(key, 11), 0)
    base = jax.random.normal(first_key, (2, GROUPS, PLEN, KVW), jnp.float32)
    result = jnp.clip(base, -6.0, 6.0)
    return result.astype(jnp.bfloat16)


def draw_lengths(key, part):
    first_key, second_key = jax.random.split(jax.random.fold_in(key, 23), 2)
    base = jax.random.randint(first_key, (REQS,), 0, SUF + 1, dtype=jnp.int32)
    picks = jax.random.permutation(second_key, REQS)
    base = base.at[picks[0]].set(SUF)
    return base.astype(jnp.int32)


def draw_owners(key, part):
    shuffled = jax.random.permutation(jax.random.fold_in(key, 37), GROUPS)
    return shuffled.astype(jnp.int32)


def touch_ends(values, stream_key, low, largest):
    longest = values.shape.index(max(values.shape))
    spots = []
    for shift in (0, 1):
        where = [jax.random.randint(jax.random.fold_in(stream_key, axis), (), 0, length) for axis, length in enumerate(values.shape)]
        where[longest] = (where[longest] + shift) % values.shape[longest]
        spots.append(tuple(where))
    return values.at[spots[0]].set(low).at[spots[1]].set(largest)


def levels(key, extent, pieces, least, largest):
    def one(dim, shards_of):
        heights = jax.random.uniform(jax.random.fold_in(jax.random.fold_in(key, 6), dim), (shards_of,), jnp.float32, least / len(pieces), largest / len(pieces))
        return jnp.repeat(jnp.exp(heights), extent[dim] // shards_of).reshape((-1,) + (1,) * (len(extent) - dim - 1))

    gain = one(*pieces[0])
    for cut in pieces[1:]:
        gain = gain * one(*cut)
    return gain


def rank_bounds(amount, slope):
    loads = [(1 << 20) // math.isqrt(rank ** slope) + 1 for rank in range(1, amount + 1)]
    width = 1 + sum(loads) // (1 << 30)
    return np.cumsum(np.array([max(1, weight // width) for weight in loads]))


def skewed_ids(stream_key, dims, amount, lean):
    grid = rank_bounds(amount, lean)
    pick = jax.random.randint(jax.random.fold_in(stream_key, 1), dims, 0, int(grid[amount - 1]))
    rank = jnp.searchsorted(jnp.asarray(grid, jnp.int32), pick, side="right")
    return jax.random.permutation(jax.random.fold_in(stream_key, 2), amount)[rank].astype(jnp.int32)


def bell_draw(stream_key, shape, scale, most, cuts=(), held_as=jnp.bfloat16):
    loudness = levels(stream_key, shape, cuts, -0.22, 0.18) if cuts else 1.0
    drawn = jax.random.normal(stream_key, shape, jnp.float32) * scale * loudness
    return jnp.minimum(jnp.maximum(drawn, -most), most).astype(held_as)


def setup_inputs(seed: int = 0) -> dict:
    key_list = jax.random.split(jax.random.key(seed), 15)
    return {
        "tokens": bell_draw(key_list[0], (TOKENS, D), 0.5, 3.0, ((0, 128),)),
        "attention_gain": jnp.clip(1.0 + 0.18 * jax.random.normal(key_list[1], (D,), jnp.float32), 0.099609375, 1.8984375).astype(jnp.bfloat16),
        "feed_gain": jnp.clip(1.0 + 0.18 * jax.random.normal(key_list[2], (D,), jnp.float32), 0.099609375, 1.8984375).astype(jnp.bfloat16),
        "w_query": bell_draw(key_list[3], (D, QW), (D // 9) ** -0.5, 0.4375, ((0, 8), (1, 16))),
        "w_key": bell_draw(key_list[4], (D, KVW), D ** -0.5, 0.15625, ((0, 8), (1, 16))),
        "w_value": bell_draw(key_list[5], (D, KVW), D ** -0.5, 0.15625, ((0, 8), (1, 16))),
        "w_out": bell_draw(key_list[6], (QW, D), QW ** -0.5, 0.15625, ((0, 16), (1, 8))),
        "w_gate": bell_draw(key_list[7], (D, FF), D ** -0.5, 0.15625, ((0, 8), (1, 16))),
        "w_up": bell_draw(key_list[8], (D, FF), D ** -0.5, 0.15625, ((0, 8), (1, 16))),
        "w_down": bell_draw(key_list[9], (FF, D), FF ** -0.5, 0.09375, ((0, 16), (1, 8))),
        "prefix_cache": draw_prefix_cache(jax.random.fold_in(key_list[14], 71), 0),
        "lengths": draw_lengths(jax.random.fold_in(key_list[14], 71), 0),
        "member": touch_ends(skewed_ids(key_list[12], (REQS,), GROUPS, 2), jax.random.fold_in(key_list[12], 3), 0, GROUPS - 1).astype(jnp.int32),
        "owners": draw_owners(jax.random.fold_in(key_list[14], 71), 0),
    }


rope_base = 100000.0
norm_eps = 1e-05
far_below = -1e+30

def rms_scale(row_values, norm_gain):
    numbers = row_values.astype(jnp.float32)
    mean_square = lax.optimization_barrier(jnp.mean(numbers * numbers, axis=-1, keepdims=True))
    return numbers * lax.rsqrt(mean_square + norm_eps) * norm_gain.astype(jnp.float32)

def rotate(numbers, positions):
    half_width = numbers.shape[-1] // 2
    frequency = rope_base ** (-(jnp.arange(half_width).astype(jnp.float32) * 2.0 / numbers.shape[-1]))
    angles = positions[:, None] * frequency[None, :]
    cosine = jnp.cos(angles)[:, None, :]
    sine_part = jnp.sin(angles)[:, None, :]
    lower_half = numbers[..., :half_width]
    upper_half = numbers[..., half_width:]
    return jnp.concatenate([lower_half * cosine - upper_half * sine_part, upper_half * cosine + lower_half * sine_part], axis=-1)

def rounded(numbers):
    return lax.optimization_barrier(numbers.astype(jnp.bfloat16)).astype(jnp.float32)

def reference(tokens, attention_gain, feed_gain, w_query, w_key, w_value, w_out, w_gate, w_up, w_down, prefix_cache, lengths, member, owners):
    score_scale = 1.0 / math.sqrt(HD)
    normed = rms_scale(tokens, attention_gain).astype(jnp.bfloat16)
    query_raw = jnp.dot(normed, w_query, preferred_element_type=jnp.float32)
    key_raw = jnp.dot(normed, w_key, preferred_element_type=jnp.float32)
    value_raw = jnp.dot(normed, w_value, preferred_element_type=jnp.float32)
    offsets = jnp.arange(TOKENS, dtype=jnp.int32) % SUF
    positions = (offsets + PLEN).astype(jnp.float32)
    queries = rotate(query_raw.reshape(TOKENS, HEADS, HD), positions).astype(jnp.bfloat16)
    keys = rotate(key_raw.reshape(TOKENS, KV_HEADS, HD), positions).astype(jnp.bfloat16)
    values = value_raw.astype(jnp.bfloat16)
    valid = jnp.arange(SUF, dtype=jnp.int32)[None, :] < lengths[:, None]
    valid_rows = valid.reshape(TOKENS).astype(jnp.float32)
    suffix_cache = (jnp.stack([keys.reshape(TOKENS, KVW).astype(jnp.float32), values.astype(jnp.float32)], 0) * valid_rows[None, :, None]).astype(jnp.bfloat16)
    causal = jnp.arange(SUF)[:, None] >= jnp.arange(SUF)[None, :]

    def attend(request):
        start_row = (request * SUF).astype(jnp.int32)
        query_rows = lax.dynamic_slice_in_dim(queries, start_row, SUF, 0).astype(jnp.float32)
        query_rows = query_rows.reshape(SUF, KV_HEADS, HEADS // KV_HEADS, HD)
        key_rows = lax.dynamic_slice_in_dim(keys, start_row, SUF, 0).astype(jnp.float32)
        value_rows = lax.dynamic_slice_in_dim(values, start_row, SUF, 0).astype(jnp.float32).reshape(SUF, KV_HEADS, HD)
        slot_index = owners[member[request]].astype(jnp.int32)
        prefix_keys = lax.dynamic_index_in_dim(prefix_cache[0], slot_index, 0, keepdims=False).astype(jnp.float32).reshape(PLEN, KV_HEADS, HD)
        prefix_values = lax.dynamic_index_in_dim(prefix_cache[1], slot_index, 0, keepdims=False).astype(jnp.float32).reshape(PLEN, KV_HEADS, HD)
        prefix_scores = jnp.einsum('ikgd,jkd->kgij', query_rows, prefix_keys) * score_scale
        prefix_top = lax.optimization_barrier(jnp.max(prefix_scores, axis=-1))
        prefix_exp = jnp.exp(prefix_scores - prefix_top[..., None])
        prefix_total = lax.optimization_barrier(jnp.sum(prefix_exp, axis=-1))
        prefix_sum = jnp.einsum('kgij,jkd->kgid', rounded(prefix_exp), prefix_values)
        suffix_scores = jnp.einsum('ikgd,jkd->kgij', query_rows, key_rows) * score_scale
        allowed = causal & (jnp.arange(SUF, dtype=jnp.int32)[None, :] < lengths[request])
        masked = jnp.where(allowed, suffix_scores, far_below)
        row_top = jnp.maximum(prefix_top, lax.optimization_barrier(jnp.max(masked, axis=-1)))
        carried = jnp.exp(prefix_top - row_top)
        suffix_exp = jnp.where(allowed, jnp.exp(masked - row_top[..., None]), 0.0)
        row_total = carried * prefix_total + lax.optimization_barrier(jnp.sum(suffix_exp, axis=-1))
        row_sum = carried[..., None] * prefix_sum + jnp.einsum('kgij,jkd->kgid', rounded(suffix_exp), value_rows)
        head_output = (row_sum / row_total[..., None]).astype(jnp.bfloat16)
        return head_output.transpose(2, 0, 1, 3).reshape(SUF, QW)
    attended = lax.map(attend, jnp.arange(REQS, dtype=jnp.int32)).reshape(TOKENS, QW)
    block_width = QW // N_MDL
    attention = jnp.zeros((TOKENS, D), jnp.float32)
    for block in range(N_MDL):
        part_sum = jnp.dot(attended[:, block * block_width:(block + 1) * block_width], w_out[block * block_width:(block + 1) * block_width], preferred_element_type=jnp.float32)
        attention = attention + rounded(part_sum)
    residual = (tokens.astype(jnp.float32) + attention).astype(jnp.bfloat16)
    normed_mid = rms_scale(residual, feed_gain).astype(jnp.bfloat16)
    gate_value = jnp.dot(normed_mid, w_gate, preferred_element_type=jnp.float32)
    up_value = jnp.dot(normed_mid, w_up, preferred_element_type=jnp.float32)
    activation = (jax.nn.silu(gate_value) * up_value).astype(jnp.bfloat16)
    unit_width = FF // N_MDL
    feed = jnp.zeros((TOKENS, D), jnp.float32)
    for block in range(N_MDL):
        part_sum = jnp.dot(activation[:, block * unit_width:(block + 1) * unit_width], w_down[block * unit_width:(block + 1) * unit_width], preferred_element_type=jnp.float32)
        feed = feed + rounded(part_sum)
    hidden = ((residual.astype(jnp.float32) + feed) * valid_rows[:, None]).astype(jnp.bfloat16)
    return (hidden, suffix_cache)
```

```python
import functools
import math

import jax
import jax.numpy as jnp
from jax import lax
from jax.experimental import pallas as pl
from jax.experimental.pallas import tpu as pltpu
from jax.sharding import PartitionSpec as P

HD = 96
HALF = 48
SUF = 512
rope_base = 100000.0
norm_eps = 1e-05
MESH = pl.DeviceIdType.MESH
LOG2E = 1.4426950408889634


def places():
    req = lax.axis_index("req")
    mdl = lax.axis_index("mdl")
    return req, mdl


class Spread:
    def __init__(self, own, block, piece, ring, pair, dev, partner, send, recv):
        self.own, self.block, self.piece = own, block, piece
        self.u, self.v, self.dev, self.partner = ring, pair, dev, partner
        self.send, self.recv, self.made = send, recv, []

    def copy(self, index, src, dst, device):
        made = pltpu.make_async_remote_copy(
            src_ref=src,
            dst_ref=dst,
            send_sem=self.send.at[index],
            recv_sem=self.recv.at[index],
            device_id=device,
            device_id_type=MESH,
        )
        made.start()
        self.made.append(made)
        return made

    def at(self, du, flip):
        return self.block(lax.rem(self.u + du, 4), 1 - self.v if flip else self.v)

    def ring_dev(self, du):
        return self.dev(lax.rem(self.u + du, 4), self.v)

    def start(self):
        here = self.at(0, False)
        self.pair_copy = self.copy(0, self.own, here, self.dev(self.u, 1 - self.v))
        self.up = self.copy(1, self.own, here, self.ring_dev(1))
        self.down = self.copy(2, self.own, here, self.ring_dev(3))
        self.own_p = self.copy(3, self.own, here, self.partner)

    def pair_arrived(self):
        self.pair_copy.wait_recv()
        other = self.at(0, True)
        self.up2 = self.copy(4, other, other, self.ring_dev(1))
        self.down2 = self.copy(5, other, other, self.ring_dev(3))
        self.copy(6, other, other, self.partner)

    def ring_arrived(self, flip):
        base = 7 + 4 * flip
        (self.up2 if flip else self.up).wait_recv()
        low = self.at(3, flip)
        a = self.copy(base, self.piece(low, 0), self.piece(low, 0), self.ring_dev(1))
        (self.down2 if flip else self.down).wait_recv()
        high = self.at(1, flip)
        b = self.copy(base + 1, self.piece(high, 1), self.piece(high, 1), self.ring_dev(3))
        self.copy(base + 2, low, low, self.partner)
        self.copy(base + 3, high, high, self.partner)
        if flip:
            self.far2 = (a, b)
        else:
            self.far = (a, b)

    def far_arrived(self, flip):
        base = 15 + 2 * flip
        for h, made in enumerate(self.far2 if flip else self.far):
            made.wait_recv()
            place = self.piece(self.at(2, flip), h)
            self.copy(base + h, place, place, self.partner)

    def finish(self):
        self.awaited = [
            self.pair_copy, self.up, self.down, self.up2, self.down2, *self.far, *self.far2
        ]
        for made in self.made:
            made.wait_send()
        for made in self.made:
            if all(made is not other for other in self.awaited):
                made.wait_recv()


SPREAD_SEMS = 19


def gather_kernel(kv_in, tok_in, kv_out, tok_out, kv_send, kv_recv, tok_send, tok_recv, local_sem):
    req, mdl = places()
    x, yh = req // 2, lax.rem(req, 2)
    z, yl, core = mdl // 4, lax.rem(mdl // 2, 2), lax.rem(mdl, 2)
    partner = {"req": req, "mdl": z * 4 + yl * 2 + 1 - core}
    rows = pl.ds(pl.multiple_of(core * HALF, HALF), HALF)

    def kv_dev(u, v):
        return {"req": u * 2 + v, "mdl": mdl}

    def tok_dev(u, v):
        return {"req": req, "mdl": u * 4 + v * 2 + core}

    barrier = pltpu.get_barrier_semaphore()
    peers = [
        partner,
        kv_dev(x, 1 - yh),
        kv_dev(lax.rem(x + 1, 4), yh),
        kv_dev(lax.rem(x + 3, 4), yh),
        tok_dev(z, 1 - yl),
        tok_dev(lax.rem(z + 1, 4), yl),
        tok_dev(lax.rem(z + 3, 4), yl),
    ]
    for peer in peers:
        pl.semaphore_signal(barrier, inc=1, device_id=peer, device_id_type=MESH)
    pl.semaphore_wait(barrier, len(peers))

    kv = Spread(
        kv_in,
        lambda u, v: kv_out.at[u * 2 + v, :, rows, :],
        lambda ref, h: ref.at[h],
        x, yh, kv_dev, partner, kv_send, kv_recv,
    )
    tok = Spread(
        tok_in,
        lambda u, v: tok_out.at[u * 4 + v * 2 + core],
        lambda ref, h: ref.at[pl.ds(64 * h, 64)],
        z, yl, tok_dev, partner, tok_send, tok_recv,
    )
    tok.start()
    kv.start()
    keep_kv = pltpu.make_async_copy(kv_in, kv.at(0, False), local_sem.at[0])
    keep_tok = pltpu.make_async_copy(tok_in, tok.at(0, False), local_sem.at[1])
    keep_kv.start()
    keep_tok.start()
    tok.pair_arrived()
    tok.ring_arrived(False)
    kv.ring_arrived(False)
    tok.ring_arrived(True)
    kv.pair_arrived()
    tok.far_arrived(False)
    tok.far_arrived(True)
    kv.far_arrived(False)
    kv.ring_arrived(True)
    kv.far_arrived(True)
    keep_kv.wait()
    keep_tok.wait()
    tok.finish()
    kv.finish()


def gather(kv_own, tokens):
    width = tokens.shape[1]
    return pl.pallas_call(
        gather_kernel,
        out_shape=(
            jax.ShapeDtypeStruct((8, 2, HD, kv_own.shape[2]), jnp.bfloat16),
            jax.ShapeDtypeStruct((16, tokens.shape[0], width), jnp.bfloat16),
        ),
        in_specs=[pl.BlockSpec(memory_space=pltpu.VMEM)] * 2,
        out_specs=[pl.BlockSpec(memory_space=pl.ANY)] * 2,
        scratch_shapes=[pltpu.SemaphoreType.DMA((SPREAD_SEMS,))] * 4
        + [pltpu.SemaphoreType.DMA((2,))],
        compiler_params=pltpu.CompilerParams(collective_id=0, has_side_effects=True),
        name="gather_kernel",
    )(kv_own, tokens)


def attend_kernel(
    slots, lens, tok_ref, gain_ref, w_ref, cos_ref, sin_ref, kv_ref, att_ref, cache_ref, kv_width
):
    request = pl.program_id(0)
    length = lens[request]
    core = lens[4]
    numbers = tok_ref[...].astype(jnp.float32)
    scale = lax.rsqrt(jnp.mean(numbers * numbers, axis=-1, keepdims=True) + norm_eps)
    normed = (numbers * scale * gain_ref[...].astype(jnp.float32)).astype(jnp.bfloat16)
    projected = lax.dot_general(
        w_ref[...], normed, (((1,), (1,)), ((), ())), preferred_element_type=jnp.float32
    )
    cosine, sine = cos_ref[...], sin_ref[...]

    def rotate(block):
        low, high = block[:HALF], block[HALF:]
        return jnp.concatenate(
            [low * cosine - high * sine, high * cosine + low * sine], axis=0
        )

    query = jnp.transpose(rotate(projected[:HD])).astype(jnp.bfloat16)
    keys_wide = rotate(projected[HD : 2 * HD])
    values_wide = projected[2 * HD :]
    keys = keys_wide.astype(jnp.bfloat16)
    values = values_wide.astype(jnp.bfloat16)
    live = (lax.broadcasted_iota(jnp.int32, (HALF, SUF), 1) < length).astype(jnp.float32)
    first = core == 0
    cache_ref[0] = (
        jnp.where(first, keys_wide[:HALF], keys_wide[HALF:]) * live
    ).astype(jnp.bfloat16)
    cache_ref[1] = (
        jnp.where(first, values_wide[:HALF], values_wide[HALF:]) * live
    ).astype(jnp.bfloat16)

    factor = LOG2E / math.sqrt(HD)
    top = total = summed = None
    chunk = 1024
    pieces = [
        (kv_ref[0, 0, :, j : j + chunk], kv_ref[0, 1, :, j : j + chunk], False)
        for j in range(0, kv_width, chunk)
    ] + [(keys, values, True)]
    for key_part, value_part, own in pieces:
        scores = jnp.dot(query, key_part, preferred_element_type=jnp.float32)
        if own:
            row = lax.broadcasted_iota(jnp.int32, scores.shape, 0)
            column = lax.broadcasted_iota(jnp.int32, scores.shape, 1)
            allowed = (column <= row) & (column < length)
            scores = jnp.where(allowed, scores, -1e30)
        part_top = jnp.max(scores, axis=-1, keepdims=True)
        new_top = part_top if top is None else jnp.maximum(top, part_top)
        weights = jnp.exp2((scores - new_top) * factor)
        if own:
            weights = jnp.where(allowed, weights, 0.0)
        part_total = jnp.sum(weights, axis=-1, keepdims=True)
        part_sum = lax.dot_general(
            weights.astype(jnp.bfloat16),
            value_part,
            (((1,), (1,)), ((), ())),
            preferred_element_type=jnp.float32,
        )
        if top is None:
            total, summed = part_total, part_sum
        else:
            carried = jnp.exp2((top - new_top) * factor)
            total = total * carried + part_total
            summed = summed * carried + part_sum
        top = new_top
    att_ref[0] = jnp.transpose(summed / total).astype(jnp.bfloat16)


def attend(slots, lens, tokens, gain, weights, cosine, sine, kv_all):
    requests = 4
    width = tokens.shape[1]
    kv_width = kv_all.shape[3]
    whole = lambda r, *_: (0, 0)
    spec = pltpu.PrefetchScalarGridSpec(
        num_scalar_prefetch=2,
        grid=(requests,),
        in_specs=[
            pl.BlockSpec((SUF, width), lambda r, *_: (r, 0)),
            pl.BlockSpec((1, width), whole),
            pl.BlockSpec(weights.shape, whole),
            pl.BlockSpec((HALF, SUF), whole),
            pl.BlockSpec((HALF, SUF), whole),
            pl.BlockSpec((1, 2, HD, kv_width), lambda r, slots, lens: (slots[r], 0, 0, 0)),
        ],
        out_specs=[
            pl.BlockSpec((1, HD, SUF), lambda r, *_: (r, 0, 0)),
            pl.BlockSpec((2, HALF, SUF), lambda r, *_: (0, 0, r)),
        ],
    )
    return pl.pallas_call(
        functools.partial(attend_kernel, kv_width=kv_width),
        grid_spec=spec,
        out_shape=(
            jax.ShapeDtypeStruct((requests, HD, SUF), jnp.bfloat16),
            jax.ShapeDtypeStruct((2, HALF, requests * SUF), jnp.bfloat16),
        ),
        compiler_params=pltpu.CompilerParams(
            dimension_semantics=("arbitrary",), vmem_limit_bytes=60 << 20
        ),
        cost_estimate=pl.CostEstimate(
            flops=6_000_000_000, bytes_accessed=20_000_000, transcendentals=10_000_000
        ),
        name="attend_kernel",
    )(slots, lens, tokens, gain, weights, cosine, sine, kv_all)


def feed_kernel(
    att_in, tok_in, gain_ref, wo_hbm, wm_hbm, out_ref,
    att, wo, wm, rows_all, part, from_pair, sums, relay, plain, joined, to_relay,
    a2a_send, a2a_recv, send, recv, w_sem,
):
    req, mdl = places()
    z, yl, core = mdl // 4, lax.rem(mdl // 2, 2), lax.rem(mdl, 2)

    def peer(du, flip=False):
        other = 1 - core if flip else core
        return {"req": req, "mdl": lax.rem(z + du, 4) * 4 + yl * 2 + other}

    barrier = pltpu.get_barrier_semaphore()
    for step in range(1, 16):
        pl.semaphore_signal(
            barrier,
            inc=1,
            device_id={"req": req, "mdl": lax.rem(mdl + step, 16)},
            device_id_type=MESH,
        )
    fetch = [pltpu.make_async_copy(wo_hbm, wo, w_sem.at[0])]
    for block in range(2):
        for kind in range(3):
            fetch.append(
                pltpu.make_async_copy(
                    wm_hbm.at[:, block, kind], wm.at[block, kind], w_sem.at[1 + 3 * block + kind]
                )
            )
    for made in fetch:
        made.start()
    pl.semaphore_wait(barrier, 15)

    def remote(src, dst, device, sends, recvs, index):
        made = pltpu.make_async_remote_copy(
            src_ref=src,
            dst_ref=dst,
            send_sem=sends.at[index],
            recv_sem=recvs.at[index],
            device_id=device,
            device_id_type=MESH,
        )
        made.start()
        return made

    exchange = []
    for step in range(1, 16):
        target = lax.rem(mdl + step, 16)
        columns = pl.ds(pl.multiple_of(lax.rem(target, 4) * 128, 128), 128)
        exchange.append(
            remote(
                att_in.at[target // 4, :, columns],
                att.at[mdl],
                {"req": req, "mdl": target},
                a2a_send,
                a2a_recv,
                step - 1,
            )
        )
    columns = pl.ds(pl.multiple_of(lax.rem(mdl, 4) * 128, 128), 128)
    att[mdl] = att_in[z, :, columns]
    for made in exchange:
        made.wait_recv()
    fetch[0].wait()
    width = tok_in.shape[1]
    attended = jnp.transpose(att[...].reshape(16 * HD, 128))
    own_rows = rows_all.at[z, core]
    for column in range(0, width, 512):
        here = slice(column, column + 512)
        attention = jnp.dot(attended, wo[:, here], preferred_element_type=jnp.float32)
        own_rows[:, here] = (tok_in[:, here].astype(jnp.float32) + attention).astype(jnp.bfloat16)

    made = []

    def go(src, dst, device, index):
        copy = remote(src, dst, device, send, recv, index)
        made.append(copy)
        return copy

    up = go(own_rows, own_rows, peer(1), 0)
    down = go(own_rows, own_rows, peer(3), 1)
    across = go(own_rows, own_rows, peer(0, True), 2)
    for copy in fetch[1:]:
        copy.wait()

    def feed(slot, du):
        there = rows_all.at[lax.rem(z + du, 4)]
        numbers = there[...].reshape(256, width).astype(jnp.float32)
        scale = lax.rsqrt(jnp.mean(numbers * numbers, axis=-1, keepdims=True) + norm_eps)
        normed = (numbers * scale * gain_ref[...].astype(jnp.float32)).astype(jnp.bfloat16)
        active = []
        for block in range(2):
            gate = jnp.dot(
                normed,
                wm[block, 0].reshape(width, 256),
                preferred_element_type=jnp.float32,
            )
            lift = jnp.dot(
                normed,
                wm[block, 1].reshape(width, 256),
                preferred_element_type=jnp.float32,
            )
            active.append((gate / (1.0 + jnp.exp(-gate)) * lift).astype(jnp.bfloat16))
        for column in range(0, width, 384):
            parts = [
                lax.dot_general(
                    active[block],
                    wm[block, 2].reshape(width, 256)[column : column + 384],
                    (((1,), (1,)), ((), ())),
                    preferred_element_type=jnp.float32,
                )
                for block in range(2)
            ]
            part[slot, :, :, column : column + 384] = (
                (parts[0] + parts[1]).astype(jnp.bfloat16).reshape(2, 128, 384)
            )
        return go(part.at[slot, 1 - core], from_pair.at[slot], peer(0, True), 3 + slot)

    def pair_sum(slot, copy):
        copy.wait_recv()
        sums[slot] = part[slot, core].astype(jnp.float32) + from_pair[slot].astype(jnp.float32)

    across.wait_recv()
    pair0 = feed(0, 0)
    up.wait_recv()
    low = rows_all.at[lax.rem(z + 3, 4), core]
    far_a = go(low.at[pl.ds(0, 64)], low.at[pl.ds(0, 64)], peer(1), 7)
    low_p = go(low, low, peer(0, True), 8)
    down.wait_recv()
    high = rows_all.at[lax.rem(z + 1, 4), core]
    far_b = go(high.at[pl.ds(64, 64)], high.at[pl.ds(64, 64)], peer(3), 9)
    high_p = go(high, high, peer(0, True), 10)
    low_p.wait_recv()
    pair3 = feed(3, 3)
    high_p.wait_recv()
    pair1 = feed(1, 1)
    far = rows_all.at[lax.rem(z + 2, 4), core]
    far_a.wait_recv()
    far_pa = go(far.at[pl.ds(0, 64)], far.at[pl.ds(0, 64)], peer(0, True), 11)
    far_b.wait_recv()
    far_pb = go(far.at[pl.ds(64, 64)], far.at[pl.ds(64, 64)], peer(0, True), 12)
    pair_sum(3, pair3)
    plain[0] = sums[3, 0:64].astype(jnp.bfloat16)
    plain_a = go(plain.at[0], plain.at[2], peer(3), 13)
    pair_sum(1, pair1)
    plain[1] = sums[1, 64:128].astype(jnp.bfloat16)
    plain_b = go(plain.at[1], plain.at[3], peer(1), 14)
    far_pa.wait_recv()
    far_pb.wait_recv()
    pair2 = feed(2, 2)
    pair_sum(2, pair2)
    to_relay[...] = sums[2].astype(jnp.bfloat16)
    relay_a = go(to_relay.at[pl.ds(0, 64)], relay.at[0], peer(1), 15)
    relay_b = go(to_relay.at[pl.ds(64, 64)], relay.at[1], peer(3), 16)
    pair_sum(0, pair0)
    relay_a.wait_recv()
    joined[0] = (sums[1, 0:64] + relay[0].astype(jnp.float32)).astype(jnp.bfloat16)
    joined_a = go(joined.at[0], joined.at[2], peer(1), 17)
    relay_b.wait_recv()
    joined[1] = (sums[3, 64:128] + relay[1].astype(jnp.float32)).astype(jnp.bfloat16)
    joined_b = go(joined.at[1], joined.at[3], peer(3), 18)
    plain_a.wait_recv()
    plain_b.wait_recv()
    joined_a.wait_recv()
    joined_b.wait_recv()
    for h in range(2):
        here = slice(64 * h, 64 * h + 64)
        feed_sum = (
            sums[0, here]
            + plain[2 + h].astype(jnp.float32)
            + joined[2 + h].astype(jnp.float32)
        )
        out_ref[here, :] = (own_rows[here, :].astype(jnp.float32) + feed_sum).astype(jnp.bfloat16)
    for copy in exchange:
        copy.wait_send()
    for copy in made:
        copy.wait_send()


def feed_forward(att, tokens, gain, w_out, w_mlp):
    rows, width = tokens.shape
    vmem = pl.BlockSpec(memory_space=pltpu.VMEM)
    anywhere = pl.BlockSpec(memory_space=pl.ANY)
    bf16, f32 = jnp.bfloat16, jnp.float32
    return pl.pallas_call(
        feed_kernel,
        out_shape=jax.ShapeDtypeStruct((rows, width), bf16),
        in_specs=[vmem, vmem, vmem, anywhere, anywhere],
        out_specs=vmem,
        scratch_shapes=[
            pltpu.VMEM((16, HD, 128), bf16),
            pltpu.VMEM((width, width), bf16),
            pltpu.VMEM((2, 3, 8, 192, 256), bf16),
            pltpu.VMEM((4, 2, rows, width), bf16),
            pltpu.VMEM((4, 2, rows, width), bf16),
            pltpu.VMEM((4, rows, width), bf16),
            pltpu.VMEM((4, rows, width), f32),
            pltpu.VMEM((2, 64, width), bf16),
            pltpu.VMEM((4, 64, width), bf16),
            pltpu.VMEM((4, 64, width), bf16),
            pltpu.VMEM((rows, width), bf16),
            pltpu.SemaphoreType.DMA((15,)),
            pltpu.SemaphoreType.DMA((15,)),
            pltpu.SemaphoreType.DMA((19,)),
            pltpu.SemaphoreType.DMA((19,)),
            pltpu.SemaphoreType.DMA((7,)),
        ],
        compiler_params=pltpu.CompilerParams(
            collective_id=1, has_side_effects=True, vmem_limit_bytes=60 << 20
        ),
        name="feed_kernel",
    )(att, tokens, gain, w_out, w_mlp)


def local(
    tokens,
    attention_gain,
    feed_gain,
    w_query,
    w_key,
    w_value,
    w_out,
    w_gate,
    w_up,
    w_down,
    prefix_cache,
    lengths,
    member,
    owners,
):
    req, mdl = places()
    core = mdl % 2
    low_half = core == 0
    prefix_length = prefix_cache.shape[2]
    kv_own = prefix_cache[:, 0].transpose(0, 2, 1)
    own_kv = jnp.stack([w_key, w_value], axis=0)
    swap = [(m, m ^ 1) for m in range(16)]
    other_kv = lax.ppermute(own_kv, "mdl", swap)
    even = jnp.where(low_half, own_kv, other_kv)
    odd = jnp.where(low_half, other_kv, own_kv)
    packed = jnp.concatenate([w_query, even[0], odd[0], even[1], odd[1]], axis=1)
    w_qkv = lax.all_gather(packed, "req", axis=0, tiled=True).T
    mlp_own = jnp.stack([w_gate, w_up, w_down.T], axis=0)
    groups = [
        [r * 16 + z * 4 + y * 2 + c for r in range(8) for y in range(2)]
        for z in range(4)
        for c in range(2)
    ]
    w_mlp = lax.all_gather(mlp_own, ("req", "mdl"), axis_index_groups=groups).reshape(
        8, 2, 3, 192, 256
    )
    w_out_rows = lax.all_gather(w_out, "req", axis=1, tiled=True)
    w_out_all = lax.all_gather(w_out_rows, "mdl", axis=0, tiled=True)

    kv_all, tok_all = gather(kv_own, tokens)

    half = HD // 2
    frequency = rope_base ** (-(jnp.arange(half).astype(jnp.float32) * 2.0 / HD))
    positions = (jnp.arange(SUF, dtype=jnp.int32) + prefix_length).astype(jnp.float32)
    angles = positions[:, None] * frequency[None, :]
    local_lengths = lax.dynamic_slice_in_dim(lengths, req * 4, 4)
    local_members = lax.dynamic_slice_in_dim(member, req * 4, 4)
    group_numbers = jnp.arange(owners.shape[0], dtype=jnp.int32)
    slots = jnp.sum(
        jnp.where(local_members[:, None] == group_numbers[None, :], owners[None, :], 0), axis=1
    )
    lens = jnp.concatenate([local_lengths, core[None].astype(jnp.int32)])
    att, cache = attend(
        slots,
        lens,
        tok_all.reshape(16 * tokens.shape[0], tokens.shape[1]),
        attention_gain[None, :],
        w_qkv,
        jnp.cos(angles).T,
        jnp.sin(angles).T,
        kv_all,
    )
    hidden = feed_forward(att, tokens, feed_gain[None, :], w_out_all, w_mlp)
    own_offset = (mdl % 4) * tokens.shape[0] + jnp.arange(tokens.shape[0], dtype=jnp.int32)
    own_length = lax.dynamic_index_in_dim(local_lengths, mdl // 4, keepdims=False)
    own_valid = own_offset < own_length
    hidden = (hidden.astype(jnp.float32) * own_valid[:, None].astype(jnp.float32)).astype(
        jnp.bfloat16
    )
    return (hidden, cache.transpose(0, 2, 1))


def solution(mesh):
    placed = (
        P(("req", "mdl"), None),
        P(),
        P(),
        P("req", "mdl"),
        P("req", "mdl"),
        P("req", "mdl"),
        P("mdl", "req"),
        P("req", "mdl"),
        P("req", "mdl"),
        P("mdl", "req"),
        P(None, "req", None, "mdl"),
        P(),
        P(),
        P(),
    )
    return jax.shard_map(
        local,
        mesh=mesh,
        in_specs=placed,
        out_specs=(P(("req", "mdl"), None), P(None, "req", "mdl")),
        check_vma=False,
    )
```

```python
import functools
import math

import jax
import jax.numpy as jnp
import numpy as np
from jax import lax
from jax.experimental import pallas as pl
from jax.experimental.pallas import tpu as pltpu
from jax.sharding import PartitionSpec as P

HD = 96
HALF = 48
SUF = 512
rope_base = 100000.0
norm_eps = 1e-05
MESH = pl.DeviceIdType.MESH
LOG2E = 1.4426950408889634


def places():
    req = lax.axis_index("req")
    mdl = lax.axis_index("mdl")
    return req, mdl


class Hub:
    def __init__(self, send, recv):
        self.send, self.recv, self.made, self.pending = send, recv, [], []

    def copy(self, src, dst, device, awaited=True):
        index = len(self.made)
        made = pltpu.make_async_remote_copy(
            src_ref=src,
            dst_ref=dst,
            send_sem=self.send.at[index],
            recv_sem=self.recv.at[index],
            device_id=device,
            device_id_type=MESH,
        )
        made.start()
        self.made.append(made)
        if not awaited:
            self.pending.append(made)
        return made

    def finish(self):
        for made in self.pending:
            made.wait_recv()
        for made in self.made:
            made.wait_send()


class Ring:
    def __init__(self, hub, region, piece, dev, u):
        self.hub, self.region, self.piece, self.dev = hub, region, piece, dev
        self.here, self.up_to, self.down_to, self.opposite = (
            u, lax.rem(u + 1, 4), lax.rem(u + 3, 4), lax.rem(u + 2, 4)
        )

    def start(self, src=None):
        block = self.region(self.here)
        src = block if src is None else src
        self.up = self.hub.copy(src, block, self.dev(self.up_to))
        self.down = self.hub.copy(src, block, self.dev(self.down_to))

    def arrive(self):
        self.up.wait_recv()
        low = self.piece(self.down_to, 0)
        self.far_low = self.hub.copy(low, low, self.dev(self.up_to))
        self.down.wait_recv()
        high = self.piece(self.up_to, 1)
        self.far_high = self.hub.copy(high, high, self.dev(self.down_to))

    def finish(self):
        self.far_low.wait_recv()
        self.far_high.wait_recv()

    def share(self, u, device):
        block = self.region(u)
        self.hub.copy(block, block, device, awaited=False)


class Spread:
    def __init__(self, hub, own, block, piece, u, v, dev, partner):
        self.hub, self.own, self.partner = hub, own, partner
        self.here, self.other = block(u, v), block(u, 1 - v)
        self.pair_dev = dev(u, 1 - v)

        def ring(w):
            return Ring(
                hub,
                lambda p: block(p, w),
                lambda p, h: piece(block(p, w), h),
                lambda p: dev(p, v),
                u,
            )

        self.rings = (ring(v), ring(1 - v))

    def start_pair(self):
        self.pair = self.hub.copy(self.own, self.here, self.pair_dev)

    def start_ring(self):
        self.rings[0].start(self.own)
        self.hub.copy(self.own, self.here, self.partner, awaited=False)

    def pair_arrived(self):
        self.pair.wait_recv()
        self.rings[1].start()
        self.hub.copy(self.other, self.other, self.partner, awaited=False)

    def ring_arrived(self, which):
        ring = self.rings[which]
        ring.arrive()
        ring.share(ring.down_to, self.partner)
        ring.share(ring.up_to, self.partner)

    def far_arrived(self, which):
        ring = self.rings[which]
        ring.finish()
        ring.share(ring.opposite, self.partner)


SEMS = 96


def gather_kernel(
    kv_in, tok_in, wq_in, wk_in, wv_in, wo_in, wg_in, wu_in, wd_in,
    kv_out, tok_out, wqkv_out, wo_out, wm_out,
    pack, send, recv, local_sem,
):
    req, mdl = places()
    x, yh = req // 2, lax.rem(req, 2)
    z, yl, core = mdl // 4, lax.rem(mdl // 2, 2), lax.rem(mdl, 2)
    y = yh * 2 + yl
    partner = {"req": req, "mdl": z * 4 + yl * 2 + 1 - core}
    rows = pl.ds(pl.multiple_of(core * HALF, HALF), HALF)

    def kv_dev(u, v):
        return {"req": u * 2 + v, "mdl": mdl}

    def tok_dev(u, v):
        return {"req": req, "mdl": u * 4 + v * 2 + core}

    def x_dev(u):
        return kv_dev(u, yh)

    def y_dev(u):
        return {"req": x * 2 + u // 2, "mdl": z * 4 + lax.rem(u, 2) * 2 + core}

    def z_dev(u):
        return tok_dev(u, yl)

    keep = []

    def store(src, dst):
        made = pltpu.make_async_copy(src, dst, local_sem.at[len(keep)])
        made.start()
        keep.append(made)

    for kind, ref in enumerate((wg_in, wu_in, wd_in)):
        store(ref, wm_out.at[x, yh, yl, kind])
    store(wo_in, wo_out.at[z, core, x, yh, yl])
    store(kv_in, kv_out.at[req, :, rows, :])
    store(tok_in, tok_out.at[mdl])
    pack[:, 0:HD] = wq_in[...]
    pack[:, HD : HD + HALF] = jnp.transpose(wk_in[...])
    pack[:, HD + HALF : 2 * HD] = jnp.transpose(wv_in[...])

    barrier = pltpu.get_barrier_semaphore()
    peers = [partner, kv_dev(x, 1 - yh)] + [
        dev(lax.rem(place + step, 4))
        for dev, place in ((x_dev, x), (y_dev, y), (z_dev, z))
        for step in (1, 3)
    ]
    for peer in peers:
        pl.semaphore_signal(barrier, inc=1, device_id=peer, device_id_type=MESH)
    pl.semaphore_wait(barrier, len(peers))

    hub = Hub(send, recv)
    kv = Spread(
        hub, kv_in,
        lambda u, v: kv_out.at[u * 2 + v, :, rows, :],
        lambda ref, h: ref.at[h],
        x, yh, kv_dev, partner,
    )
    tok = Spread(
        hub, tok_in,
        lambda u, v: tok_out.at[u * 4 + v * 2 + core],
        lambda ref, h: ref.at[pl.ds(64 * h, 64)],
        z, yl, tok_dev, partner,
    )
    qkv = Spread(
        hub, pack,
        lambda u, v: wqkv_out.at[u * 2 + v, core],
        lambda ref, h: ref.at[pl.ds(96 * h, 96)],
        x, yh, kv_dev, partner,
    )
    wo_x = Ring(
        hub,
        lambda u: wo_out.at[z, core, u, yh, yl],
        lambda u, h: wo_out.at[z, core, u, yh, yl, pl.ds(48 * h, 48)],
        x_dev, x,
    )
    wo_y = Ring(
        hub,
        lambda u: wo_out.at[z, core, :, u // 2, lax.rem(u, 2)],
        lambda u, h: wo_out.at[z, core, pl.ds(2 * h, 2), u // 2, lax.rem(u, 2)],
        y_dev, y,
    )
    wo_z = Ring(
        hub,
        lambda u: wo_out.at[u, core],
        lambda u, h: wo_out.at[u, core, pl.ds(2 * h, 2)],
        z_dev, z,
    )
    wm_x = Ring(
        hub,
        lambda u: wm_out.at[u, yh, yl],
        lambda u, h: wm_out.at[u, yh, yl, :, pl.ds(96 * h, 96)],
        x_dev, x,
    )

    def wm_ring(step):
        u_x = lax.rem(x + step, 4)
        return Ring(
            hub,
            lambda u: wm_out.at[u_x, u // 2, lax.rem(u, 2)],
            lambda u, h: wm_out.at[u_x, u // 2, lax.rem(u, 2), :, pl.ds(96 * h, 96)],
            y_dev, y,
        )

    wm_y = [wm_ring(step) for step in range(4)]

    kv.start_pair()
    tok.start_pair()
    for made in keep[:4]:
        made.wait()
    wm_x.start()
    wo_x.start(wo_in)
    qkv.start_pair()
    qkv.start_ring()
    tok.start_ring()
    wm_y[0].start()
    kv.start_ring()
    store(pack, wqkv_out.at[req, core])

    wm_x.arrive()
    wm_y[3].start()
    wm_y[1].start()
    wo_x.arrive()
    tok.pair_arrived()
    qkv.ring_arrived(0)
    qkv.pair_arrived()
    tok.ring_arrived(0)
    wo_x.finish()
    wo_y.start()
    kv.ring_arrived(0)
    wm_x.finish()
    wm_y[2].start()
    kv.pair_arrived()
    wm_y[0].arrive()
    tok.ring_arrived(1)
    qkv.far_arrived(0)
    qkv.ring_arrived(1)
    wo_y.arrive()
    tok.far_arrived(0)
    kv.far_arrived(0)
    wo_y.finish()
    wo_z.start()
    wo_z.share(z, partner)
    wm_y[3].arrive()
    wm_y[1].arrive()
    tok.far_arrived(1)
    qkv.far_arrived(1)
    kv.ring_arrived(1)
    wo_z.arrive()
    wo_z.share(wo_z.down_to, partner)
    wo_z.share(wo_z.up_to, partner)
    wm_y[2].arrive()
    wo_z.finish()
    wo_z.share(wo_z.opposite, partner)
    kv.far_arrived(1)
    for ring in wm_y:
        ring.finish()
    for made in keep[4:]:
        made.wait()
    hub.finish()


def gather(kv_own, tokens, w_query, w_key, w_value, w_out, w_gate, w_up, w_down):
    rows, width = tokens.shape
    shape = lambda *dims: jax.ShapeDtypeStruct(dims, jnp.bfloat16)
    return pl.pallas_call(
        gather_kernel,
        out_shape=(
            shape(8, 2, HD, kv_own.shape[2]),
            shape(16, rows, width),
            shape(8, 2, 192, 192),
            shape(4, 2, 4, 2, 2, 96, 192),
            shape(4, 2, 2, 3, 192, 256),
        ),
        in_specs=[pl.BlockSpec(memory_space=pltpu.VMEM)] * 9,
        out_specs=[pl.BlockSpec(memory_space=pl.ANY)] * 5,
        scratch_shapes=[
            pltpu.VMEM((192, 192), jnp.bfloat16),
            pltpu.SemaphoreType.DMA((SEMS,)),
            pltpu.SemaphoreType.DMA((SEMS,)),
            pltpu.SemaphoreType.DMA((8,)),
        ],
        compiler_params=pltpu.CompilerParams(collective_id=0, has_side_effects=True),
        name="gather_kernel",
    )(kv_own, tokens, w_query, w_key, w_value, w_out, w_gate, w_up, w_down)


def attend_kernel(
    lengths, member, owners, place,
    tok_ref, gain_ref, w_ref, cos_ref, sin_ref, kv_ref, att_ref, cache_ref, kv_width,
):
    length = lengths[place[0] * 4 + pl.program_id(0)]
    core = place[1]
    width = tok_ref.shape[1]
    numbers = tok_ref[...].astype(jnp.float32)
    scale = lax.rsqrt(jnp.mean(numbers * numbers, axis=-1, keepdims=True) + norm_eps)
    normed = (numbers * scale * gain_ref[...].astype(jnp.float32)).astype(jnp.bfloat16)
    halves = [
        jnp.transpose(
            jnp.dot(normed, w_ref[:, c].reshape(width, 192), preferred_element_type=jnp.float32)
        )
        for c in range(2)
    ]
    first = core == 0
    cosine, sine = cos_ref[...], sin_ref[...]

    def rotate(block):
        low, high = block[:HALF], block[HALF:]
        return jnp.concatenate(
            [low * cosine - high * sine, high * cosine + low * sine], axis=0
        )

    query_raw = jnp.where(first, halves[0][:HD], halves[1][:HD])
    query = jnp.transpose(rotate(query_raw)).astype(jnp.bfloat16)
    keys_wide = rotate(jnp.concatenate([half[HD : HD + HALF] for half in halves], axis=0))
    values_wide = jnp.concatenate([half[HD + HALF :] for half in halves], axis=0)
    keys = keys_wide.astype(jnp.bfloat16)
    values = values_wide.astype(jnp.bfloat16)
    live = (lax.broadcasted_iota(jnp.int32, (HALF, SUF), 1) < length).astype(jnp.float32)
    cache_ref[0] = (
        jnp.where(first, keys_wide[:HALF], keys_wide[HALF:]) * live
    ).astype(jnp.bfloat16)
    cache_ref[1] = (
        jnp.where(first, values_wide[:HALF], values_wide[HALF:]) * live
    ).astype(jnp.bfloat16)

    factor = LOG2E / math.sqrt(HD)
    top = total = summed = None
    chunk = 1024
    pieces = [
        (kv_ref[0, 0, :, j : j + chunk], kv_ref[0, 1, :, j : j + chunk], False)
        for j in range(0, kv_width, chunk)
    ] + [(keys, values, True)]
    for key_part, value_part, own in pieces:
        scores = jnp.dot(query, key_part, preferred_element_type=jnp.float32)
        if own:
            row = lax.broadcasted_iota(jnp.int32, scores.shape, 0)
            column = lax.broadcasted_iota(jnp.int32, scores.shape, 1)
            allowed = (column <= row) & (column < length)
            scores = jnp.where(allowed, scores, -1e30)
        part_top = jnp.max(scores, axis=-1, keepdims=True)
        new_top = part_top if top is None else jnp.maximum(top, part_top)
        weights = jnp.exp2((scores - new_top) * factor)
        if own:
            weights = jnp.where(allowed, weights, 0.0)
        part_total = jnp.sum(weights, axis=-1, keepdims=True)
        part_sum = lax.dot_general(
            weights.astype(jnp.bfloat16),
            value_part,
            (((1,), (1,)), ((), ())),
            preferred_element_type=jnp.float32,
        )
        if top is None:
            total, summed = part_total, part_sum
        else:
            carried = jnp.exp2((top - new_top) * factor)
            total = total * carried + part_total
            summed = summed * carried + part_sum
        top = new_top
    att_ref[0] = jnp.transpose(summed / total).astype(jnp.bfloat16)


def attend(lengths, member, owners, place, tokens, gain, weights, cosine, sine, kv_all):
    requests = 4
    width = tokens.shape[1]
    kv_width = kv_all.shape[3]
    whole = lambda r, *_: (0, 0)

    def slot(r, lengths, member, owners, place):
        return (owners[member[place[0] * 4 + r]], 0, 0, 0)

    spec = pltpu.PrefetchScalarGridSpec(
        num_scalar_prefetch=4,
        grid=(requests,),
        in_specs=[
            pl.BlockSpec((SUF, width), lambda r, *_: (r, 0)),
            pl.BlockSpec((1, width), whole),
            pl.BlockSpec(weights.shape, lambda r, *_: (0, 0, 0, 0)),
            pl.BlockSpec((HALF, SUF), whole),
            pl.BlockSpec((HALF, SUF), whole),
            pl.BlockSpec((1, 2, HD, kv_width), slot),
        ],
        out_specs=[
            pl.BlockSpec((1, HD, SUF), lambda r, *_: (r, 0, 0)),
            pl.BlockSpec((2, HALF, SUF), lambda r, *_: (0, 0, r)),
        ],
    )
    return pl.pallas_call(
        functools.partial(attend_kernel, kv_width=kv_width),
        grid_spec=spec,
        out_shape=(
            jax.ShapeDtypeStruct((requests, HD, SUF), jnp.bfloat16),
            jax.ShapeDtypeStruct((2, HALF, requests * SUF), jnp.bfloat16),
        ),
        compiler_params=pltpu.CompilerParams(
            dimension_semantics=("arbitrary",), vmem_limit_bytes=60 << 20
        ),
        cost_estimate=pl.CostEstimate(
            flops=6_000_000_000, bytes_accessed=20_000_000, transcendentals=10_000_000
        ),
        name="attend_kernel",
    )(lengths, member, owners, place, tokens, gain, weights, cosine, sine, kv_all)


def feed_kernel(
    att_in, tok_in, gain_ref, wo_hbm, wm_hbm, out_ref,
    att, wo, wm, rows_all, part, from_pair, sums, relay, plain, joined, to_relay,
    a2a_send, a2a_recv, send, recv, w_sem,
):
    req, mdl = places()
    z, yl, core = mdl // 4, lax.rem(mdl // 2, 2), lax.rem(mdl, 2)

    def peer(du, flip=False):
        other = 1 - core if flip else core
        return {"req": req, "mdl": lax.rem(z + du, 4) * 4 + yl * 2 + other}

    barrier = pltpu.get_barrier_semaphore()
    for step in range(1, 16):
        pl.semaphore_signal(
            barrier,
            inc=1,
            device_id={"req": req, "mdl": lax.rem(mdl + step, 16)},
            device_id_type=MESH,
        )
    fetch = []
    for u in range(4):
        for c in range(2):
            fetch.append(
                pltpu.make_async_copy(
                    wo_hbm.at[u, c], wo.at[:, :, u, :, c], w_sem.at[len(fetch)]
                )
            )
    for block in range(2):
        for kind in range(3):
            fetch.append(
                pltpu.make_async_copy(
                    wm_hbm.at[:, :, block, kind], wm.at[block, kind], w_sem.at[len(fetch)]
                )
            )
    for made in fetch:
        made.start()
    pl.semaphore_wait(barrier, 15)

    def remote(src, dst, device, sends, recvs, index):
        made = pltpu.make_async_remote_copy(
            src_ref=src,
            dst_ref=dst,
            send_sem=sends.at[index],
            recv_sem=recvs.at[index],
            device_id=device,
            device_id_type=MESH,
        )
        made.start()
        return made

    exchange = []
    for step in range(1, 16):
        target = lax.rem(mdl + step, 16)
        columns = pl.ds(pl.multiple_of(lax.rem(target, 4) * 128, 128), 128)
        exchange.append(
            remote(
                att_in.at[target // 4, :, columns],
                att.at[mdl],
                {"req": req, "mdl": target},
                a2a_send,
                a2a_recv,
                step - 1,
            )
        )
    columns = pl.ds(pl.multiple_of(lax.rem(mdl, 4) * 128, 128), 128)
    att[mdl] = att_in[z, :, columns]
    for made in exchange:
        made.wait_recv()
    for made in fetch[:8]:
        made.wait()
    width = tok_in.shape[1]
    attended = jnp.transpose(att[...].reshape(16 * HD, 128))
    own_rows = rows_all.at[z, core]
    for u in range(4):
        attention = jnp.concatenate(
            [
                jnp.dot(
                    attended, wo[u, v].reshape(16 * HD, 192), preferred_element_type=jnp.float32
                )
                for v in range(2)
            ],
            axis=1,
        )
        here = slice(384 * u, 384 * u + 384)
        own_rows[:, here] = (tok_in[:, here].astype(jnp.float32) + attention).astype(jnp.bfloat16)

    made = []

    def go(src, dst, device, index):
        copy = remote(src, dst, device, send, recv, index)
        made.append(copy)
        return copy

    up = go(own_rows, own_rows, peer(1), 0)
    down = go(own_rows, own_rows, peer(3), 1)
    across = go(own_rows, own_rows, peer(0, True), 2)
    for copy in fetch[8:]:
        copy.wait()

    def feed(slot, du):
        there = rows_all.at[lax.rem(z + du, 4)]
        numbers = there[...].reshape(256, width).astype(jnp.float32)
        scale = lax.rsqrt(jnp.mean(numbers * numbers, axis=-1, keepdims=True) + norm_eps)
        normed = (numbers * scale * gain_ref[...].astype(jnp.float32)).astype(jnp.bfloat16)
        active = []
        for block in range(2):
            gate = jnp.dot(
                normed,
                wm[block, 0].reshape(width, 256),
                preferred_element_type=jnp.float32,
            )
            lift = jnp.dot(
                normed,
                wm[block, 1].reshape(width, 256),
                preferred_element_type=jnp.float32,
            )
            active.append((gate / (1.0 + jnp.exp(-gate)) * lift).astype(jnp.bfloat16))
        for column in range(0, width, 384):
            parts = [
                lax.dot_general(
                    active[block],
                    wm[block, 2].reshape(width, 256)[column : column + 384],
                    (((1,), (1,)), ((), ())),
                    preferred_element_type=jnp.float32,
                )
                for block in range(2)
            ]
            part[slot, :, :, column : column + 384] = (
                (parts[0] + parts[1]).astype(jnp.bfloat16).reshape(2, 128, 384)
            )
        return go(part.at[slot, 1 - core], from_pair.at[slot], peer(0, True), 3 + slot)

    def pair_sum(slot, copy):
        copy.wait_recv()
        sums[slot] = part[slot, core].astype(jnp.float32) + from_pair[slot].astype(jnp.float32)

    across.wait_recv()
    pair0 = feed(0, 0)
    up.wait_recv()
    low = rows_all.at[lax.rem(z + 3, 4), core]
    far_a = go(low.at[pl.ds(0, 64)], low.at[pl.ds(0, 64)], peer(1), 7)
    low_p = go(low, low, peer(0, True), 8)
    down.wait_recv()
    high = rows_all.at[lax.rem(z + 1, 4), core]
    far_b = go(high.at[pl.ds(64, 64)], high.at[pl.ds(64, 64)], peer(3), 9)
    high_p = go(high, high, peer(0, True), 10)
    low_p.wait_recv()
    pair3 = feed(3, 3)
    high_p.wait_recv()
    pair1 = feed(1, 1)
    far = rows_all.at[lax.rem(z + 2, 4), core]
    far_a.wait_recv()
    far_pa = go(far.at[pl.ds(0, 64)], far.at[pl.ds(0, 64)], peer(0, True), 11)
    far_b.wait_recv()
    far_pb = go(far.at[pl.ds(64, 64)], far.at[pl.ds(64, 64)], peer(0, True), 12)
    pair_sum(3, pair3)
    plain[0] = sums[3, 0:64].astype(jnp.bfloat16)
    plain_a = go(plain.at[0], plain.at[2], peer(3), 13)
    pair_sum(1, pair1)
    plain[1] = sums[1, 64:128].astype(jnp.bfloat16)
    plain_b = go(plain.at[1], plain.at[3], peer(1), 14)
    far_pa.wait_recv()
    far_pb.wait_recv()
    pair2 = feed(2, 2)
    pair_sum(2, pair2)
    to_relay[...] = sums[2].astype(jnp.bfloat16)
    relay_a = go(to_relay.at[pl.ds(0, 64)], relay.at[0], peer(1), 15)
    relay_b = go(to_relay.at[pl.ds(64, 64)], relay.at[1], peer(3), 16)
    pair_sum(0, pair0)
    relay_a.wait_recv()
    joined[0] = (sums[1, 0:64] + relay[0].astype(jnp.float32)).astype(jnp.bfloat16)
    joined_a = go(joined.at[0], joined.at[2], peer(1), 17)
    relay_b.wait_recv()
    joined[1] = (sums[3, 64:128] + relay[1].astype(jnp.float32)).astype(jnp.bfloat16)
    joined_b = go(joined.at[1], joined.at[3], peer(3), 18)
    plain_a.wait_recv()
    plain_b.wait_recv()
    joined_a.wait_recv()
    joined_b.wait_recv()
    for h in range(2):
        here = slice(64 * h, 64 * h + 64)
        feed_sum = (
            sums[0, here]
            + plain[2 + h].astype(jnp.float32)
            + joined[2 + h].astype(jnp.float32)
        )
        out_ref[here, :] = (own_rows[here, :].astype(jnp.float32) + feed_sum).astype(jnp.bfloat16)
    for copy in exchange:
        copy.wait_send()
    for copy in made:
        copy.wait_send()


def feed_forward(att, tokens, gain, w_out, w_mlp):
    rows, width = tokens.shape
    vmem = pl.BlockSpec(memory_space=pltpu.VMEM)
    anywhere = pl.BlockSpec(memory_space=pl.ANY)
    bf16, f32 = jnp.bfloat16, jnp.float32
    return pl.pallas_call(
        feed_kernel,
        out_shape=jax.ShapeDtypeStruct((rows, width), bf16),
        in_specs=[vmem, vmem, vmem, anywhere, anywhere],
        out_specs=vmem,
        scratch_shapes=[
            pltpu.VMEM((16, HD, 128), bf16),
            pltpu.VMEM((4, 2, 4, 2, 2, HD, 192), bf16),
            pltpu.VMEM((2, 3, 4, 2, 192, 256), bf16),
            pltpu.VMEM((4, 2, rows, width), bf16),
            pltpu.VMEM((4, 2, rows, width), bf16),
            pltpu.VMEM((4, rows, width), bf16),
            pltpu.VMEM((4, rows, width), f32),
            pltpu.VMEM((2, 64, width), bf16),
            pltpu.VMEM((4, 64, width), bf16),
            pltpu.VMEM((4, 64, width), bf16),
            pltpu.VMEM((rows, width), bf16),
            pltpu.SemaphoreType.DMA((15,)),
            pltpu.SemaphoreType.DMA((15,)),
            pltpu.SemaphoreType.DMA((19,)),
            pltpu.SemaphoreType.DMA((19,)),
            pltpu.SemaphoreType.DMA((14,)),
        ],
        compiler_params=pltpu.CompilerParams(
            collective_id=1, has_side_effects=True, vmem_limit_bytes=60 << 20
        ),
        name="feed_kernel",
    )(att, tokens, gain, w_out, w_mlp)


def local(
    tokens,
    attention_gain,
    feed_gain,
    w_query,
    w_key,
    w_value,
    w_out,
    w_gate,
    w_up,
    w_down,
    prefix_cache,
    lengths,
    member,
    owners,
):
    req, mdl = places()
    prefix_length = prefix_cache.shape[2]
    kv_all, tok_all, w_qkv, w_out_all, w_mlp = gather(
        prefix_cache[:, 0].transpose(0, 2, 1),
        tokens,
        w_query,
        w_key.T,
        w_value.T,
        w_out,
        w_gate,
        w_up,
        w_down.T,
    )
    half = np.arange(HD // 2).astype(np.float32)
    frequency = np.float32(rope_base) ** (-(half * np.float32(2.0) / np.float32(HD)))
    positions = (np.arange(SUF) + prefix_length).astype(np.float32)
    angles = (frequency[:, None] * positions[None, :]).astype(np.float64)
    place = jnp.stack([req, mdl % 2]).astype(jnp.int32)
    att, cache = attend(
        lengths,
        member,
        owners,
        place,
        tok_all.reshape(16 * tokens.shape[0], tokens.shape[1]),
        attention_gain[None, :],
        w_qkv,
        np.cos(angles).astype(np.float32),
        np.sin(angles).astype(np.float32),
        kv_all,
    )
    hidden = feed_forward(att, tokens, feed_gain[None, :], w_out_all, w_mlp)
    own_offset = (mdl % 4) * tokens.shape[0] + jnp.arange(tokens.shape[0], dtype=jnp.int32)
    own_length = lax.dynamic_index_in_dim(lengths, req * 4 + mdl // 4, keepdims=False)
    own_valid = own_offset < own_length
    hidden = (hidden.astype(jnp.float32) * own_valid[:, None].astype(jnp.float32)).astype(
        jnp.bfloat16
    )
    return (hidden, cache.transpose(0, 2, 1))


def solution(mesh):
    placed = (
        P(("req", "mdl"), None),
        P(),
        P(),
        P("req", "mdl"),
        P("req", "mdl"),
        P("req", "mdl"),
        P("mdl", "req"),
        P("req", "mdl"),
        P("req", "mdl"),
        P("mdl", "req"),
        P(None, "req", None, "mdl"),
        P(),
        P(),
        P(),
    )
    return jax.shard_map(
        local,
        mesh=mesh,
        in_specs=placed,
        out_specs=(P(("req", "mdl"), None), P(None, "req", "mdl")),
        check_vma=False,
    )
```

```python
import math

import jax
import jax.numpy as jnp
import numpy as np
from jax import lax
from jax.experimental import pallas as pl
from jax.experimental.pallas import tpu as pltpu
from jax.sharding import PartitionSpec as P

HD = 96
HALF = 48
SUF = 512
rope_base = 100000.0
norm_eps = 1e-05
MESH = pl.DeviceIdType.MESH
LOG2E = 1.4426950408889634


def places():
    req = lax.axis_index("req")
    mdl = lax.axis_index("mdl")
    return req, mdl


class Hub:
    def __init__(self, send, recv):
        self.send, self.recv, self.made, self.pending = send, recv, [], []

    def copy(self, src, dst, device, awaited=True):
        index = len(self.made)
        made = pltpu.make_async_remote_copy(
            src_ref=src,
            dst_ref=dst,
            send_sem=self.send.at[index],
            recv_sem=self.recv.at[index],
            device_id=device,
            device_id_type=MESH,
        )
        made.start()
        self.made.append(made)
        if not awaited:
            self.pending.append(made)
        return made

    def shared(self):
        for made in self.pending:
            made.wait_recv()
        self.pending = []

    def finish(self):
        self.shared()
        for made in self.made:
            made.wait_send()


class Ring:
    def __init__(self, hub, region, piece, dev, u):
        self.hub, self.region, self.piece, self.dev = hub, region, piece, dev
        self.here, self.up_to, self.down_to, self.opposite = (
            u, lax.rem(u + 1, 4), lax.rem(u + 3, 4), lax.rem(u + 2, 4)
        )

    def start(self, src=None):
        block = self.region(self.here)
        src = block if src is None else src
        self.up = self.hub.copy(src, block, self.dev(self.up_to))
        self.down = self.hub.copy(src, block, self.dev(self.down_to))

    def arrive(self):
        self.up.wait_recv()
        low = self.piece(self.down_to, 0)
        self.far_low = self.hub.copy(low, low, self.dev(self.up_to))
        self.down.wait_recv()
        high = self.piece(self.up_to, 1)
        self.far_high = self.hub.copy(high, high, self.dev(self.down_to))

    def finish(self):
        self.far_low.wait_recv()
        self.far_high.wait_recv()

    def share(self, u, device):
        block = self.region(u)
        return self.hub.copy(block, block, device, awaited=False)


class Spread:
    def __init__(self, hub, own, block, piece, u, v, dev, partner):
        self.hub, self.own, self.partner = hub, own, partner
        self.here, self.other = block(u, v), block(u, 1 - v)
        self.pair_dev = dev(u, 1 - v)
        self.handed = []

        def ring(w):
            return Ring(
                hub,
                lambda p: block(p, w),
                lambda p, h: piece(block(p, w), h),
                lambda p: dev(p, v),
                u,
            )

        self.rings = (ring(v), ring(1 - v))

    def start_pair(self):
        self.pair = self.hub.copy(self.own, self.here, self.pair_dev)

    def start_ring(self):
        self.rings[0].start(self.own)
        self.handed.append(self.hub.copy(self.own, self.here, self.partner))

    def pair_arrived(self):
        self.pair.wait_recv()
        self.rings[1].start()
        self.handed.append(self.hub.copy(self.other, self.other, self.partner))

    def ring_arrived(self, which):
        ring = self.rings[which]
        ring.arrive()
        self.hand(ring, ring.down_to)
        self.hand(ring, ring.up_to)

    def far_arrived(self, which):
        ring = self.rings[which]
        ring.finish()
        self.hand(ring, ring.opposite)

    def hand(self, ring, u):
        block = ring.region(u)
        self.handed.append(self.hub.copy(block, block, self.partner))

    def shared(self):
        for made in self.handed:
            made.wait_recv()


SEMS = 116


def layer_kernel(
    lengths, member, owners,
    kv_in, tok_in, wq_in, wk_in, wv_in, wo_in, wg_in, wu_in, wd_in,
    gain_ref, feed_gain_ref, cos_ref, sin_ref,
    out_ref, cache_ref,
    kv_all, tok_all, wqkv, wo, wm, pack, query, keys, values, att_out, att,
    rows_all, part, from_pair, sums, relay, plain, joined, to_relay,
    send, recv, a2a_send, a2a_recv, local_sem,
):
    req, mdl = places()
    x, yh = req // 2, lax.rem(req, 2)
    z, yl, core = mdl // 4, lax.rem(mdl // 2, 2), lax.rem(mdl, 2)
    y = yh * 2 + yl
    quarter = lax.rem(mdl, 4)
    width = tok_in.shape[1]
    partner = {"req": req, "mdl": z * 4 + yl * 2 + 1 - core}
    rows = pl.ds(pl.multiple_of(core * HALF, HALF), HALF)

    def kv_dev(u, v):
        return {"req": u * 2 + v, "mdl": mdl}

    def tok_dev(u, v):
        return {"req": req, "mdl": u * 4 + v * 2 + core}

    def x_dev(u):
        return kv_dev(u, yh)

    def y_dev(u):
        return {"req": x * 2 + u // 2, "mdl": z * 4 + lax.rem(u, 2) * 2 + core}

    def z_dev(u):
        return tok_dev(u, yl)

    barrier = pltpu.get_barrier_semaphore()
    peers = [kv_dev(x, 1 - yh)]
    peers += [x_dev(lax.rem(x + step, 4)) for step in (1, 3)]
    peers += [y_dev(lax.rem(y + step, 4)) for step in (1, 3)]
    peers += [{"req": req, "mdl": lax.rem(mdl + step, 16)} for step in range(1, 16)]
    for peer in peers:
        pl.semaphore_signal(barrier, inc=1, device_id=peer, device_id_type=MESH)

    keep = []

    def store(src, dst):
        made = pltpu.make_async_copy(src, dst, local_sem.at[len(keep)])
        made.start()
        keep.append(made)

    store(wo_in, wo.at[z, core, x, yh, yl])
    for kind, ref in enumerate((wg_in, wu_in, wd_in)):
        store(ref, wm.at[x, yh, yl, kind])
    store(kv_in, kv_all.at[req, :, rows, :])
    store(tok_in, tok_all.at[mdl])
    pack[:, 0:HD] = wq_in[...]
    pack[:, HD : HD + HALF] = jnp.transpose(wk_in[...])
    pack[:, HD + HALF : 2 * HD] = jnp.transpose(wv_in[...])
    pl.semaphore_wait(barrier, len(peers))

    hub = Hub(send, recv)
    kv = Spread(
        hub, kv_in,
        lambda u, v: kv_all.at[u * 2 + v, :, rows, :],
        lambda ref, h: ref.at[h],
        x, yh, kv_dev, partner,
    )
    tok = Spread(
        hub, tok_in,
        lambda u, v: tok_all.at[u * 4 + v * 2 + core],
        lambda ref, h: ref.at[pl.ds(64 * h, 64)],
        z, yl, tok_dev, partner,
    )
    qkv = Spread(
        hub, pack,
        lambda u, v: wqkv.at[u * 2 + v, core],
        lambda ref, h: ref.at[pl.ds(96 * h, 96)],
        x, yh, kv_dev, partner,
    )
    wo_x = Ring(
        hub,
        lambda u: wo.at[z, core, u, yh, yl],
        lambda u, h: wo.at[z, core, u, yh, yl, pl.ds(48 * h, 48)],
        x_dev, x,
    )
    wo_y = Ring(
        hub,
        lambda u: wo.at[z, core, :, u // 2, lax.rem(u, 2)],
        lambda u, h: wo.at[z, core, pl.ds(2 * h, 2), u // 2, lax.rem(u, 2)],
        y_dev, y,
    )
    wo_z = Ring(
        hub,
        lambda u: wo.at[u, core],
        lambda u, h: wo.at[u, core, pl.ds(2 * h, 2)],
        z_dev, z,
    )
    wm_x = Ring(
        hub,
        lambda u: wm.at[u, yh, yl],
        lambda u, h: wm.at[u, yh, yl, :, pl.ds(96 * h, 96)],
        x_dev, x,
    )

    def wm_ring(step):
        u_x = lax.rem(x + step, 4)
        return Ring(
            hub,
            lambda u: wm.at[u_x, u // 2, lax.rem(u, 2)],
            lambda u, h: wm.at[u_x, u // 2, lax.rem(u, 2), :, pl.ds(96 * h, 96)],
            y_dev, y,
        )

    wm_y = [wm_ring(step) for step in range(4)]

    def project(r, carry):
        numbers = tok_all[pl.ds(4 * r, 4)].reshape(SUF, width).astype(jnp.float32)
        scale = lax.rsqrt(jnp.mean(numbers * numbers, axis=-1, keepdims=True) + norm_eps)
        normed = (numbers * scale * gain_ref[...].astype(jnp.float32)).astype(jnp.bfloat16)
        halves = [
            jnp.transpose(
                jnp.dot(
                    normed, wqkv[:, c].reshape(width, 192), preferred_element_type=jnp.float32
                )
            )
            for c in range(2)
        ]
        cosine, sine = cos_ref[...], sin_ref[...]

        def rotate(block):
            low, high = block[:HALF], block[HALF:]
            return jnp.concatenate(
                [low * cosine - high * sine, high * cosine + low * sine], axis=0
            )

        first = core == 0
        query_raw = jnp.where(first, halves[0][:HD], halves[1][:HD])
        keys_wide = rotate(jnp.concatenate([half[HD : HD + HALF] for half in halves], axis=0))
        values_wide = jnp.concatenate([half[HD + HALF :] for half in halves], axis=0)
        query[r] = jnp.transpose(rotate(query_raw)).astype(jnp.bfloat16)
        keys[r] = keys_wide.astype(jnp.bfloat16)
        values[r] = values_wide.astype(jnp.bfloat16)
        length = lengths[req * 4 + r]
        live = (lax.broadcasted_iota(jnp.int32, (HALF, SUF), 1) < length).astype(jnp.float32)
        columns = pl.ds(pl.multiple_of(r * SUF, SUF), SUF)
        for kind, wide in enumerate((keys_wide, values_wide)):
            own = jnp.where(first, wide[:HALF], wide[HALF:])
            cache_ref[kind, :, columns] = (own * live).astype(jnp.bfloat16)
        return carry

    def attend(i, carry):
        r = lax.rem(z + 1 + i, 4)
        length = lengths[req * 4 + r]
        slot = owners[member[req * 4 + r]]
        factor = LOG2E / math.sqrt(HD)
        chunk = 1024
        top = total = summed = None
        for j in range(0, kv_all.shape[3] + 1, chunk):
            own = j == kv_all.shape[3]
            if own:
                key_part, value_part = keys[r], values[r]
            else:
                key_part = kv_all[slot, 0, :, j : j + chunk]
                value_part = kv_all[slot, 1, :, j : j + chunk]
            scores = jnp.dot(query[r], key_part, preferred_element_type=jnp.float32)
            if own:
                row = lax.broadcasted_iota(jnp.int32, scores.shape, 0)
                column = lax.broadcasted_iota(jnp.int32, scores.shape, 1)
                allowed = (column <= row) & (column < length)
                scores = jnp.where(allowed, scores, -1e30)
            part_top = jnp.max(scores, axis=-1, keepdims=True)
            new_top = part_top if top is None else jnp.maximum(top, part_top)
            weights = jnp.exp2((scores - new_top) * factor)
            if own:
                weights = jnp.where(allowed, weights, 0.0)
            part_total = jnp.sum(weights, axis=-1, keepdims=True)
            part_sum = lax.dot_general(
                weights.astype(jnp.bfloat16),
                value_part,
                (((1,), (1,)), ((), ())),
                preferred_element_type=jnp.float32,
            )
            if top is None:
                total, summed = part_total, part_sum
            else:
                carried = jnp.exp2((top - new_top) * factor)
                total = total * carried + part_total
                summed = summed * carried + part_sum
            top = new_top
        att_out[r] = jnp.transpose(summed / total).astype(jnp.bfloat16)
        for j in range(4):

            @pl.when(r * 4 + j != mdl)
            def _():
                pltpu.make_async_remote_copy(
                    src_ref=att_out.at[r, :, pl.ds(128 * j, 128)],
                    dst_ref=att.at[mdl],
                    send_sem=a2a_send.at[i * 4 + j],
                    recv_sem=a2a_recv.at[i * 4 + quarter],
                    device_id={"req": req, "mdl": r * 4 + j},
                    device_id_type=MESH,
                ).start()

        return carry

    wo_x.start(wo_in)
    qkv.start_ring()
    qkv.start_pair()
    tok.start_pair()
    tok.start_ring()
    store(pack, wqkv.at[req, core])
    wo_x.arrive()
    qkv.ring_arrived(0)
    qkv.pair_arrived()
    kv.start_ring()
    wo_x.finish()
    keep[0].wait()
    wo_y.start()
    kv.start_pair()
    for made in keep[1:4]:
        made.wait()
    wm_x.start()
    wm_y[0].start()
    tok.pair_arrived()
    tok.ring_arrived(0)
    qkv.far_arrived(0)
    wo_y.arrive()
    tok.ring_arrived(1)
    kv.ring_arrived(0)
    tok.far_arrived(0)
    tok.far_arrived(1)
    wm_x.arrive()
    wm_y[3].start()
    wm_y[1].start()
    kv.pair_arrived()
    qkv.ring_arrived(1)
    wo_y.finish()
    wo_z.start()
    wo_z.share(z, partner)
    qkv.far_arrived(1)
    wm_y[0].arrive()
    for made in keep[4:]:
        made.wait()
    tok.shared()
    qkv.shared()
    lax.fori_loop(0, 4, project, 0)
    kv.far_arrived(0)
    wo_z.arrive()
    wo_z.share(wo_z.down_to, partner)
    wo_z.share(wo_z.up_to, partner)
    wm_y[3].arrive()
    wm_y[1].arrive()
    kv.ring_arrived(1)
    wm_x.finish()
    wm_y[2].start()
    wo_z.finish()
    wo_z.share(wo_z.opposite, partner)
    kv.far_arrived(1)
    kv.shared()
    lax.fori_loop(0, 4, attend, 0)
    wm_y[2].arrive()
    att[mdl] = att_out[z, :, pl.ds(pl.multiple_of(quarter * 128, 128), 128)]

    def exchange(i, j, sending):
        k = i * 4 + j
        made = pltpu.make_async_remote_copy(
            src_ref=att_out.at[0, :, pl.ds(0, 128)],
            dst_ref=att.at[j],
            send_sem=a2a_send.at[k],
            recv_sem=a2a_recv.at[k],
            device_id=partner,
            device_id_type=MESH,
        )

        def wait():
            made.wait_send() if sending else made.wait_recv()

        if i < 3:
            wait()
        else:
            pl.when(quarter != j)(wait)

    hub.shared()
    for i in range(4):
        for j in range(4):
            exchange(i, j, False)
    attended = jnp.transpose(att[...].reshape(16 * HD, 128))
    own_rows = rows_all.at[z, core]
    for u in range(4):
        attention = jnp.concatenate(
            [
                jnp.dot(
                    attended,
                    jnp.concatenate(
                        [wo[k // 4, k % 2, u, v, (k // 2) % 2] for k in range(16)], axis=0
                    ),
                    preferred_element_type=jnp.float32,
                )
                for v in range(2)
            ],
            axis=1,
        )
        here = slice(384 * u, 384 * u + 384)
        own_rows[:, here] = (tok_in[:, here].astype(jnp.float32) + attention).astype(jnp.bfloat16)

    def peer(du, flip=False):
        other = 1 - core if flip else core
        return {"req": req, "mdl": lax.rem(z + du, 4) * 4 + yl * 2 + other}

    go = hub.copy
    up = go(own_rows, own_rows, peer(1))
    down = go(own_rows, own_rows, peer(3))
    across = go(own_rows, own_rows, peer(0, True))
    for ring in wm_y:
        ring.finish()

    def feed(slot, du):
        there = rows_all.at[lax.rem(z + du, 4)]
        numbers = there[...].reshape(256, width).astype(jnp.float32)
        scale = lax.rsqrt(jnp.mean(numbers * numbers, axis=-1, keepdims=True) + norm_eps)
        normed = (numbers * scale * feed_gain_ref[...].astype(jnp.float32)).astype(jnp.bfloat16)
        active = []
        for block in range(2):
            gate = jnp.dot(
                normed,
                wm[:, :, block, 0].reshape(width, 256),
                preferred_element_type=jnp.float32,
            )
            lift = jnp.dot(
                normed,
                wm[:, :, block, 1].reshape(width, 256),
                preferred_element_type=jnp.float32,
            )
            active.append((gate / (1.0 + jnp.exp(-gate)) * lift).astype(jnp.bfloat16))
        for u in range(4):
            parts = [
                lax.dot_general(
                    active[block],
                    wm[u, :, block, 2].reshape(384, 256),
                    (((1,), (1,)), ((), ())),
                    preferred_element_type=jnp.float32,
                )
                for block in range(2)
            ]
            part[slot, :, :, 384 * u : 384 * u + 384] = (
                (parts[0] + parts[1]).astype(jnp.bfloat16).reshape(2, 128, 384)
            )
        return go(part.at[slot, 1 - core], from_pair.at[slot], peer(0, True))

    def pair_sum(slot, copy):
        copy.wait_recv()
        sums[slot] = part[slot, core].astype(jnp.float32) + from_pair[slot].astype(jnp.float32)

    across.wait_recv()
    pair0 = feed(0, 0)
    up.wait_recv()
    low = rows_all.at[lax.rem(z + 3, 4), core]
    far_a = go(low.at[pl.ds(0, 64)], low.at[pl.ds(0, 64)], peer(1))
    low_p = go(low, low, peer(0, True))
    down.wait_recv()
    high = rows_all.at[lax.rem(z + 1, 4), core]
    far_b = go(high.at[pl.ds(64, 64)], high.at[pl.ds(64, 64)], peer(3))
    high_p = go(high, high, peer(0, True))
    low_p.wait_recv()
    pair3 = feed(3, 3)
    high_p.wait_recv()
    pair1 = feed(1, 1)
    far = rows_all.at[lax.rem(z + 2, 4), core]
    far_a.wait_recv()
    far_pa = go(far.at[pl.ds(0, 64)], far.at[pl.ds(0, 64)], peer(0, True))
    far_b.wait_recv()
    far_pb = go(far.at[pl.ds(64, 64)], far.at[pl.ds(64, 64)], peer(0, True))
    pair_sum(3, pair3)
    plain[0] = sums[3, 0:64].astype(jnp.bfloat16)
    plain_a = go(plain.at[0], plain.at[2], peer(3))
    pair_sum(1, pair1)
    plain[1] = sums[1, 64:128].astype(jnp.bfloat16)
    plain_b = go(plain.at[1], plain.at[3], peer(1))
    far_pa.wait_recv()
    far_pb.wait_recv()
    pair2 = feed(2, 2)
    pair_sum(2, pair2)
    to_relay[...] = sums[2].astype(jnp.bfloat16)
    relay_a = go(to_relay.at[pl.ds(0, 64)], relay.at[0], peer(1))
    relay_b = go(to_relay.at[pl.ds(64, 64)], relay.at[1], peer(3))
    pair_sum(0, pair0)
    relay_a.wait_recv()
    joined[0] = (sums[1, 0:64] + relay[0].astype(jnp.float32)).astype(jnp.bfloat16)
    joined_a = go(joined.at[0], joined.at[2], peer(1))
    relay_b.wait_recv()
    joined[1] = (sums[3, 64:128] + relay[1].astype(jnp.float32)).astype(jnp.bfloat16)
    joined_b = go(joined.at[1], joined.at[3], peer(3))
    plain_a.wait_recv()
    plain_b.wait_recv()
    joined_a.wait_recv()
    joined_b.wait_recv()
    for h in range(2):
        here = slice(64 * h, 64 * h + 64)
        feed_sum = (
            sums[0, here]
            + plain[2 + h].astype(jnp.float32)
            + joined[2 + h].astype(jnp.float32)
        )
        out_ref[here, :] = (own_rows[here, :].astype(jnp.float32) + feed_sum).astype(jnp.bfloat16)
    for i in range(4):
        for j in range(4):
            exchange(i, j, True)
    hub.finish()


def layer(scalars, arrays):
    kv_own, tokens = arrays[:2]
    rows, width = tokens.shape
    bf16, f32 = jnp.bfloat16, jnp.float32
    vmem = pl.BlockSpec(memory_space=pltpu.VMEM)
    return pl.pallas_call(
        layer_kernel,
        out_shape=(
            jax.ShapeDtypeStruct((rows, width), bf16),
            jax.ShapeDtypeStruct((2, HALF, 4 * SUF), bf16),
        ),
        in_specs=[pl.BlockSpec(memory_space=pltpu.SMEM)] * len(scalars) + [vmem] * len(arrays),
        out_specs=[vmem] * 2,
        scratch_shapes=[
            pltpu.VMEM((8, 2, HD, kv_own.shape[2]), bf16),
            pltpu.VMEM((16, rows, width), bf16),
            pltpu.VMEM((8, 2, 192, 192), bf16),
            pltpu.VMEM((4, 2, 4, 2, 2, HD, 192), bf16),
            pltpu.VMEM((4, 2, 2, 3, 192, 256), bf16),
            pltpu.VMEM((192, 192), bf16),
            pltpu.VMEM((4, SUF, HD), bf16),
            pltpu.VMEM((4, HD, SUF), bf16),
            pltpu.VMEM((4, HD, SUF), bf16),
            pltpu.VMEM((4, HD, SUF), bf16),
            pltpu.VMEM((16, HD, 128), bf16),
            pltpu.VMEM((4, 2, rows, width), bf16),
            pltpu.VMEM((4, 2, rows, width), bf16),
            pltpu.VMEM((4, rows, width), bf16),
            pltpu.VMEM((4, rows, width), f32),
            pltpu.VMEM((2, 64, width), bf16),
            pltpu.VMEM((4, 64, width), bf16),
            pltpu.VMEM((4, 64, width), bf16),
            pltpu.VMEM((rows, width), bf16),
            pltpu.SemaphoreType.DMA((SEMS,)),
            pltpu.SemaphoreType.DMA((SEMS,)),
            pltpu.SemaphoreType.DMA((16,)),
            pltpu.SemaphoreType.DMA((16,)),
            pltpu.SemaphoreType.DMA((8,)),
        ],
        compiler_params=pltpu.CompilerParams(
            collective_id=0, has_side_effects=True, vmem_limit_bytes=67_043_328
        ),
        name="layer_kernel",
    )(*scalars, *arrays)


def local(
    tokens,
    attention_gain,
    feed_gain,
    w_query,
    w_key,
    w_value,
    w_out,
    w_gate,
    w_up,
    w_down,
    prefix_cache,
    lengths,
    member,
    owners,
):
    req, mdl = places()
    prefix_length = prefix_cache.shape[2]
    half = np.arange(HD // 2).astype(np.float32)
    frequency = np.float32(rope_base) ** (-(half * np.float32(2.0) / np.float32(HD)))
    positions = (np.arange(SUF) + prefix_length).astype(np.float32)
    angles = (frequency[:, None] * positions[None, :]).astype(np.float64)
    hidden, cache = layer(
        (lengths, member, owners),
        (
            prefix_cache[:, 0].transpose(0, 2, 1),
            tokens,
            w_query,
            w_key.T,
            w_value.T,
            w_out,
            w_gate,
            w_up,
            w_down.T,
            attention_gain[None, :],
            feed_gain[None, :],
            np.cos(angles).astype(np.float32),
            np.sin(angles).astype(np.float32),
        ),
    )
    own_offset = (mdl % 4) * tokens.shape[0] + jnp.arange(tokens.shape[0], dtype=jnp.int32)
    own_length = lax.dynamic_index_in_dim(lengths, req * 4 + mdl // 4, keepdims=False)
    own_valid = own_offset < own_length
    hidden = (hidden.astype(jnp.float32) * own_valid[:, None].astype(jnp.float32)).astype(
        jnp.bfloat16
    )
    return (hidden, cache.transpose(0, 2, 1))


def solution(mesh):
    placed = (
        P(("req", "mdl"), None),
        P(),
        P(),
        P("req", "mdl"),
        P("req", "mdl"),
        P("req", "mdl"),
        P("mdl", "req"),
        P("req", "mdl"),
        P("req", "mdl"),
        P("mdl", "req"),
        P(None, "req", None, "mdl"),
        P(),
        P(),
        P(),
    )
    return jax.shard_map(
        local,
        mesh=mesh,
        in_specs=placed,
        out_specs=(P(("req", "mdl"), None), P(None, "req", "mdl")),
        check_vma=False,
    )
```

```python
import math

import jax
import jax.numpy as jnp
import numpy as np
from jax import lax
from jax.experimental import pallas as pl
from jax.experimental.pallas import tpu as pltpu
from jax.sharding import PartitionSpec as P

HD = 96
HALF = 48
SUF = 512
rope_base = 100000.0
norm_eps = 1e-05
MESH = pl.DeviceIdType.MESH
LOG2E = 1.4426950408889634


def places():
    req = lax.axis_index("req")
    mdl = lax.axis_index("mdl")
    return req, mdl


class Hub:
    def __init__(self, send, recv):
        self.send, self.recv, self.made, self.pending = send, recv, [], []

    def copy(self, src, dst, device, awaited=True):
        index = len(self.made)
        made = pltpu.make_async_remote_copy(
            src_ref=src,
            dst_ref=dst,
            send_sem=self.send.at[index],
            recv_sem=self.recv.at[index],
            device_id=device,
            device_id_type=MESH,
        )
        made.start()
        self.made.append(made)
        if not awaited:
            self.pending.append(made)
        return made

    def shared(self):
        for made in self.pending:
            made.wait_recv()
        self.pending = []

    def finish(self):
        self.shared()
        for made in self.made:
            made.wait_send()


class Ring:
    def __init__(self, hub, region, piece, dev, u):
        self.hub, self.region, self.piece, self.dev = hub, region, piece, dev
        self.here, self.up_to, self.down_to, self.opposite = (
            u, lax.rem(u + 1, 4), lax.rem(u + 3, 4), lax.rem(u + 2, 4)
        )

    def start(self, src=None):
        block = self.region(self.here)
        src = block if src is None else src
        self.up = self.hub.copy(src, block, self.dev(self.up_to))
        self.down = self.hub.copy(src, block, self.dev(self.down_to))

    def near(self):
        self.up.wait_recv()
        self.down.wait_recv()

    def arrive(self, waited=False):
        if not waited:
            self.up.wait_recv()
        low = self.piece(self.down_to, 0)
        self.far_low = self.hub.copy(low, low, self.dev(self.up_to))
        if not waited:
            self.down.wait_recv()
        high = self.piece(self.up_to, 1)
        self.far_high = self.hub.copy(high, high, self.dev(self.down_to))

    def finish(self):
        self.far_low.wait_recv()
        self.far_high.wait_recv()

    def start_split(self, src):
        here, up, down = self.here, self.dev(self.up_to), self.dev(self.down_to)
        self.up = self.hub.copy(src.at[0], self.piece(here, 0), up)
        self.down = self.hub.copy(src.at[1], self.piece(here, 1), down)
        self.up_rest = self.hub.copy(src.at[1], self.piece(here, 1), up)
        self.down_rest = self.hub.copy(src.at[0], self.piece(here, 0), down)

    def rest(self):
        self.up_rest.wait_recv()
        self.down_rest.wait_recv()

    def share(self, u, device):
        block = self.region(u)
        return self.hub.copy(block, block, device, awaited=False)


class Direct:
    def __init__(self, hub, region, dev, u):
        self.hub, self.region, self.dev, self.here = hub, region, dev, u

    def start(self, src=None):
        block = self.region(self.here)
        src = block if src is None else src
        self.sent = [
            self.hub.copy(src, block, self.dev(lax.rem(self.here + step, 4)))
            for step in (1, 3, 2)
        ]

    def finish(self):
        for made in self.sent:
            made.wait_recv()


class Spread:
    def __init__(self, hub, own, block, piece, u, v, dev, partner):
        self.hub, self.own, self.partner = hub, own, partner
        self.here, self.other = block(u, v), block(u, 1 - v)
        self.pair_dev = dev(u, 1 - v)
        self.handed = []

        def ring(w):
            return Ring(
                hub,
                lambda p: block(p, w),
                lambda p, h: piece(block(p, w), h),
                lambda p: dev(p, v),
                u,
            )

        self.rings = (ring(v), ring(1 - v))

    def start_pair(self):
        self.pair = self.hub.copy(self.own, self.here, self.pair_dev)

    def start_ring(self):
        self.rings[0].start(self.own)
        self.handed.append(self.hub.copy(self.own, self.here, self.partner))

    def pair_arrived(self):
        self.pair.wait_recv()
        self.rings[1].start()
        self.handed.append(self.hub.copy(self.other, self.other, self.partner))

    def ring_arrived(self, which):
        ring = self.rings[which]
        ring.arrive()
        self.hand(ring, ring.down_to)
        self.hand(ring, ring.up_to)

    def far_arrived(self, which):
        ring = self.rings[which]
        ring.finish()
        self.hand(ring, ring.opposite)

    def hand(self, ring, u):
        block = ring.region(u)
        self.handed.append(self.hub.copy(block, block, self.partner))

    def shared(self):
        for made in self.handed:
            made.wait_recv()


SEMS = 130
KV_EARLY = 3072


def layer_kernel(
    lengths, member, owners,
    kv_in, tok_in, wq_in, wk_in, wv_in, wo_in, wg_in, wu_in, wd_in,
    gain_ref, feed_gain_ref, cos_ref, sin_ref,
    out_ref, cache_ref,
    kv_all, tok_all, wqkv, wo, wm, pack, query, keys, values, att_out, att,
    rows_all, part, from_pair, sums, relay, plain, joined, to_relay,
    send, recv, a2a_send, a2a_recv, local_sem,
):
    req, mdl = places()
    x, yh = req // 2, lax.rem(req, 2)
    z, yl, core = mdl // 4, lax.rem(mdl // 2, 2), lax.rem(mdl, 2)
    y = yh * 2 + yl
    quarter = lax.rem(mdl, 4)
    width = tok_in.shape[1]
    partner = {"req": req, "mdl": z * 4 + yl * 2 + 1 - core}
    rows = pl.ds(pl.multiple_of(core * HALF, HALF), HALF)

    def kv_dev(u, v):
        return {"req": u * 2 + v, "mdl": mdl}

    def tok_dev(u, v):
        return {"req": req, "mdl": u * 4 + v * 2 + core}

    def x_dev(u):
        return kv_dev(u, yh)

    def y_dev(u):
        return {"req": x * 2 + u // 2, "mdl": z * 4 + lax.rem(u, 2) * 2 + core}

    def z_dev(u):
        return tok_dev(u, yl)

    barrier = pltpu.get_barrier_semaphore()
    peers = [kv_dev(x, 1 - yh)]
    peers += [x_dev(lax.rem(x + step, 4)) for step in (1, 2, 3)]
    peers += [y_dev(lax.rem(y + step, 4)) for step in (1, 3)]
    peers += [{"req": req, "mdl": lax.rem(mdl + step, 16)} for step in range(1, 16)]
    for peer in peers:
        pl.semaphore_signal(barrier, inc=1, device_id=peer, device_id_type=MESH)

    keep = []

    def store(src, dst):
        made = pltpu.make_async_copy(src, dst, local_sem.at[len(keep)])
        made.start()
        keep.append(made)

    store(wo_in, wo.at[z, core, x, yh, yl])
    for kind, ref in enumerate((wg_in, wu_in, wd_in)):
        store(ref, wm.at[x, yh, yl, kind])
    store(kv_in, kv_all.at[req, :, rows, :])
    store(tok_in, tok_all.at[mdl])
    pack[:, 0:HD] = wq_in[...]
    pack[:, HD : HD + HALF] = jnp.transpose(wk_in[...])
    pack[:, HD + HALF : 2 * HD] = jnp.transpose(wv_in[...])
    pl.semaphore_wait(barrier, len(peers))

    hub = Hub(send, recv)
    early, late = pl.ds(0, KV_EARLY), pl.ds(KV_EARLY, kv_all.shape[3] - KV_EARLY)
    kv_ring = Ring(
        hub,
        lambda u: kv_all.at[u * 2 + yh, :, rows],
        lambda u, h: kv_all.at[u * 2 + yh, h, rows],
        x_dev, x,
    )
    kv_other = Ring(
        hub,
        lambda u: kv_all.at[u * 2 + 1 - yh, :, rows, early],
        lambda u, h: kv_all.at[u * 2 + 1 - yh, h, rows, early],
        x_dev, x,
    )
    kv_pair = kv_dev(x, 1 - yh)
    handed = []

    def hand(block):
        handed.append(hub.copy(block, block, partner))

    def cross(u):
        block = kv_all.at[u * 2 + yh, :, rows, late]
        return hub.copy(block, block, kv_pair)

    def crossed(u, made):
        made.wait_recv()
        hand(kv_all.at[u * 2 + 1 - yh, :, rows, late])

    tok = Spread(
        hub, tok_in,
        lambda u, v: tok_all.at[u * 4 + v * 2 + core],
        lambda ref, h: ref.at[pl.ds(64 * h, 64)],
        z, yl, tok_dev, partner,
    )
    qkv = Spread(
        hub, pack,
        lambda u, v: wqkv.at[u * 2 + v, core],
        lambda ref, h: ref.at[pl.ds(96 * h, 96)],
        x, yh, kv_dev, partner,
    )
    wo_x = Direct(hub, lambda u: wo.at[z, core, u, yh, yl], x_dev, x)
    wo_y = Direct(hub, lambda u: wo.at[z, core, :, u // 2, lax.rem(u, 2)], y_dev, y)
    wo_z = Ring(
        hub,
        lambda u: wo.at[u, core],
        lambda u, h: wo.at[u, core, pl.ds(2 * h, 2)],
        z_dev, z,
    )
    wm_x = Ring(
        hub,
        lambda u: wm.at[u, yh, yl],
        lambda u, h: wm.at[u, yh, yl, :, pl.ds(96 * h, 96)],
        x_dev, x,
    )

    def wm_ring(step):
        u_x = lax.rem(x + step, 4)
        return Ring(
            hub,
            lambda u: wm.at[u_x, u // 2, lax.rem(u, 2)],
            lambda u, h: wm.at[u_x, u // 2, lax.rem(u, 2), :, pl.ds(96 * h, 96)],
            y_dev, y,
        )

    wm_y = [wm_ring(step) for step in range(4)]

    def project(r, carry):
        numbers = tok_all[pl.ds(4 * r, 4)].reshape(SUF, width).astype(jnp.float32)
        scale = lax.rsqrt(jnp.mean(numbers * numbers, axis=-1, keepdims=True) + norm_eps)
        normed = (numbers * scale * gain_ref[...].astype(jnp.float32)).astype(jnp.bfloat16)
        halves = [
            jnp.transpose(
                jnp.dot(
                    normed, wqkv[:, c].reshape(width, 192), preferred_element_type=jnp.float32
                )
            )
            for c in range(2)
        ]
        cosine, sine = cos_ref[...], sin_ref[...]

        def rotate(block):
            low, high = block[:HALF], block[HALF:]
            return jnp.concatenate(
                [low * cosine - high * sine, high * cosine + low * sine], axis=0
            )

        first = core == 0
        query_raw = jnp.where(first, halves[0][:HD], halves[1][:HD])
        keys_wide = rotate(jnp.concatenate([half[HD : HD + HALF] for half in halves], axis=0))
        values_wide = jnp.concatenate([half[HD + HALF :] for half in halves], axis=0)
        query[r] = jnp.transpose(rotate(query_raw)).astype(jnp.bfloat16)
        keys[r] = keys_wide.astype(jnp.bfloat16)
        values[r] = values_wide.astype(jnp.bfloat16)
        length = lengths[req * 4 + r]
        live = (lax.broadcasted_iota(jnp.int32, (HALF, SUF), 1) < length).astype(jnp.float32)
        columns = pl.ds(pl.multiple_of(r * SUF, SUF), SUF)
        for kind, wide in enumerate((keys_wide, values_wide)):
            own = jnp.where(first, wide[:HALF], wide[HALF:])
            cache_ref[kind, :, columns] = (own * live).astype(jnp.bfloat16)
        return carry

    def attend(i, carry):
        r = lax.rem(z + 1 + i, 4)
        length = lengths[req * 4 + r]
        slot = owners[member[req * 4 + r]]
        factor = LOG2E / math.sqrt(HD)
        chunk = 1024
        top = total = summed = None
        for j in range(0, kv_all.shape[3] + 1, chunk):
            own = j == kv_all.shape[3]
            if own:
                key_part, value_part = keys[r], values[r]
            else:
                key_part = kv_all[slot, 0, :, j : j + chunk]
                value_part = kv_all[slot, 1, :, j : j + chunk]
            scores = jnp.dot(query[r], key_part, preferred_element_type=jnp.float32)
            if own:
                row = lax.broadcasted_iota(jnp.int32, scores.shape, 0)
                column = lax.broadcasted_iota(jnp.int32, scores.shape, 1)
                allowed = (column <= row) & (column < length)
                scores = jnp.where(allowed, scores, -1e30)
            part_top = jnp.max(scores, axis=-1, keepdims=True)
            new_top = part_top if top is None else jnp.maximum(top, part_top)
            weights = jnp.exp2((scores - new_top) * factor)
            if own:
                weights = jnp.where(allowed, weights, 0.0)
            part_total = jnp.sum(weights, axis=-1, keepdims=True)
            part_sum = lax.dot_general(
                weights.astype(jnp.bfloat16),
                value_part,
                (((1,), (1,)), ((), ())),
                preferred_element_type=jnp.float32,
            )
            if top is None:
                total, summed = part_total, part_sum
            else:
                carried = jnp.exp2((top - new_top) * factor)
                total = total * carried + part_total
                summed = summed * carried + part_sum
            top = new_top
        att_out[r] = jnp.transpose(summed / total).astype(jnp.bfloat16)
        for j in range(4):

            @pl.when(r * 4 + j != mdl)
            def _():
                pltpu.make_async_remote_copy(
                    src_ref=att_out.at[r, :, pl.ds(128 * j, 128)],
                    dst_ref=att.at[mdl],
                    send_sem=a2a_send.at[i * 4 + j],
                    recv_sem=a2a_recv.at[i * 4 + quarter],
                    device_id={"req": req, "mdl": r * 4 + j},
                    device_id_type=MESH,
                ).start()

        return carry

    kv_here = kv_ring.region(x)
    wo_x.start(wo_in)
    tok.start_pair()
    kv_ring.start_split(kv_in)
    tok.start_ring()
    qkv.start_pair()
    kv_over = hub.copy(kv_in, kv_here, kv_pair)
    qkv.start_ring()
    handed.append(hub.copy(kv_in, kv_here, partner))
    store(pack, wqkv.at[req, core])
    keep[0].wait()
    wo_x.finish()
    wo_y.start()
    kv_ring.arrive()
    tok.pair_arrived()
    tok.ring_arrived(0)
    qkv.pair_arrived()
    for made in keep[1:4]:
        made.wait()
    wm_x.start()
    kv_ring.rest()
    cross_low = cross(kv_ring.down_to)
    cross_high = cross(kv_ring.up_to)
    hand(kv_ring.region(kv_ring.down_to))
    hand(kv_ring.region(kv_ring.up_to))
    qkv.ring_arrived(0)
    kv_over.wait_recv()
    kv_other.start_split(kv_other.region(x))
    hand(kv_all.at[x * 2 + 1 - yh, :, rows])
    tok.ring_arrived(1)
    qkv.ring_arrived(1)
    kv_ring.finish()
    cross_far = cross(kv_ring.opposite)
    hand(kv_ring.region(kv_ring.opposite))
    wm_y[0].start()
    wo_y.finish()
    wo_z.start()
    wo_z.share(z, partner)
    wm_x.near()
    wm_y[3].start()
    wm_y[1].start()
    tok.far_arrived(0)
    tok.far_arrived(1)
    qkv.far_arrived(0)
    kv_other.arrive()
    wm_x.arrive(True)
    qkv.far_arrived(1)
    for made in keep[4:]:
        made.wait()
    tok.shared()
    qkv.shared()
    lax.fori_loop(0, 4, project, 0)
    crossed(kv_ring.down_to, cross_low)
    crossed(kv_ring.up_to, cross_high)
    kv_other.rest()
    hand(kv_other.region(kv_other.down_to))
    hand(kv_other.region(kv_other.up_to))
    crossed(kv_ring.opposite, cross_far)
    wm_y[0].arrive()
    wo_z.arrive()
    wo_z.share(wo_z.down_to, partner)
    wo_z.share(wo_z.up_to, partner)
    kv_other.finish()
    hand(kv_other.region(kv_other.opposite))
    for made in handed:
        made.wait_recv()
    attend(0, 0)
    wm_x.finish()
    wm_y[2].start()
    attend(1, 0)
    wo_z.finish()
    wo_z.share(wo_z.opposite, partner)
    wm_y[3].arrive()
    wm_y[1].arrive()
    attend(2, 0)
    attend(3, 0)
    wm_y[2].arrive()
    att[mdl] = att_out[z, :, pl.ds(pl.multiple_of(quarter * 128, 128), 128)]

    def exchange(i, j, sending):
        k = i * 4 + j
        made = pltpu.make_async_remote_copy(
            src_ref=att_out.at[0, :, pl.ds(0, 128)],
            dst_ref=att.at[j],
            send_sem=a2a_send.at[k],
            recv_sem=a2a_recv.at[k],
            device_id=partner,
            device_id_type=MESH,
        )

        def wait():
            made.wait_send() if sending else made.wait_recv()

        if i < 3:
            wait()
        else:
            pl.when(quarter != j)(wait)

    hub.shared()
    for i in range(4):
        for j in range(4):
            exchange(i, j, False)
    attended = jnp.transpose(att[...].reshape(16 * HD, 128))
    own_rows = rows_all.at[z, core]
    for u in range(4):
        attention = jnp.concatenate(
            [
                jnp.dot(
                    attended,
                    jnp.concatenate(
                        [wo[k // 4, k % 2, u, v, (k // 2) % 2] for k in range(16)], axis=0
                    ),
                    preferred_element_type=jnp.float32,
                )
                for v in range(2)
            ],
            axis=1,
        )
        here = slice(384 * u, 384 * u + 384)
        own_rows[:, here] = (tok_in[:, here].astype(jnp.float32) + attention).astype(jnp.bfloat16)

    def peer(du, flip=False):
        other = 1 - core if flip else core
        return {"req": req, "mdl": lax.rem(z + du, 4) * 4 + yl * 2 + other}

    go = hub.copy
    up = go(own_rows, own_rows, peer(1))
    down = go(own_rows, own_rows, peer(3))
    across = go(own_rows, own_rows, peer(0, True))
    for ring in wm_y:
        ring.finish()

    def feed(slot, du):
        there = rows_all.at[lax.rem(z + du, 4)]
        numbers = there[...].reshape(256, width).astype(jnp.float32)
        scale = lax.rsqrt(jnp.mean(numbers * numbers, axis=-1, keepdims=True) + norm_eps)
        normed = (numbers * scale * feed_gain_ref[...].astype(jnp.float32)).astype(jnp.bfloat16)
        active = []
        for block in range(2):
            gate = jnp.dot(
                normed,
                wm[:, :, block, 0].reshape(width, 256),
                preferred_element_type=jnp.float32,
            )
            lift = jnp.dot(
                normed,
                wm[:, :, block, 1].reshape(width, 256),
                preferred_element_type=jnp.float32,
            )
            active.append((gate / (1.0 + jnp.exp(-gate)) * lift).astype(jnp.bfloat16))
        for u in range(4):
            parts = [
                lax.dot_general(
                    active[block],
                    wm[u, :, block, 2].reshape(384, 256),
                    (((1,), (1,)), ((), ())),
                    preferred_element_type=jnp.float32,
                )
                for block in range(2)
            ]
            part[slot, :, :, 384 * u : 384 * u + 384] = (
                (parts[0] + parts[1]).astype(jnp.bfloat16).reshape(2, 128, 384)
            )
        return go(part.at[slot, 1 - core], from_pair.at[slot], peer(0, True))

    def pair_sum(slot, copy):
        copy.wait_recv()
        sums[slot] = part[slot, core].astype(jnp.float32) + from_pair[slot].astype(jnp.float32)

    across.wait_recv()
    pair0 = feed(0, 0)
    up.wait_recv()
    low = rows_all.at[lax.rem(z + 3, 4), core]
    far_a = go(low.at[pl.ds(0, 64)], low.at[pl.ds(0, 64)], peer(1))
    low_p = go(low, low, peer(0, True))
    down.wait_recv()
    high = rows_all.at[lax.rem(z + 1, 4), core]
    far_b = go(high.at[pl.ds(64, 64)], high.at[pl.ds(64, 64)], peer(3))
    high_p = go(high, high, peer(0, True))
    low_p.wait_recv()
    pair3 = feed(3, 3)
    high_p.wait_recv()
    pair1 = feed(1, 1)
    far = rows_all.at[lax.rem(z + 2, 4), core]
    far_a.wait_recv()
    far_pa = go(far.at[pl.ds(0, 64)], far.at[pl.ds(0, 64)], peer(0, True))
    far_b.wait_recv()
    far_pb = go(far.at[pl.ds(64, 64)], far.at[pl.ds(64, 64)], peer(0, True))
    pair_sum(3, pair3)
    plain[0] = sums[3, 0:64].astype(jnp.bfloat16)
    plain_a = go(plain.at[0], plain.at[2], peer(3))
    pair_sum(1, pair1)
    plain[1] = sums[1, 64:128].astype(jnp.bfloat16)
    plain_b = go(plain.at[1], plain.at[3], peer(1))
    far_pa.wait_recv()
    far_pb.wait_recv()
    pair2 = feed(2, 2)
    pair_sum(2, pair2)
    to_relay[...] = sums[2].astype(jnp.bfloat16)
    relay_a = go(to_relay.at[pl.ds(0, 64)], relay.at[0], peer(1))
    relay_b = go(to_relay.at[pl.ds(64, 64)], relay.at[1], peer(3))
    pair_sum(0, pair0)
    relay_a.wait_recv()
    joined[0] = (sums[1, 0:64] + relay[0].astype(jnp.float32)).astype(jnp.bfloat16)
    joined_a = go(joined.at[0], joined.at[2], peer(1))
    relay_b.wait_recv()
    joined[1] = (sums[3, 64:128] + relay[1].astype(jnp.float32)).astype(jnp.bfloat16)
    joined_b = go(joined.at[1], joined.at[3], peer(3))
    plain_a.wait_recv()
    plain_b.wait_recv()
    joined_a.wait_recv()
    joined_b.wait_recv()
    for h in range(2):
        here = slice(64 * h, 64 * h + 64)
        feed_sum = (
            sums[0, here]
            + plain[2 + h].astype(jnp.float32)
            + joined[2 + h].astype(jnp.float32)
        )
        out_ref[here, :] = (own_rows[here, :].astype(jnp.float32) + feed_sum).astype(jnp.bfloat16)
    for i in range(4):
        for j in range(4):
            exchange(i, j, True)
    hub.finish()


def layer(scalars, arrays):
    kv_own, tokens = arrays[:2]
    rows, width = tokens.shape
    bf16, f32 = jnp.bfloat16, jnp.float32
    vmem = pl.BlockSpec(memory_space=pltpu.VMEM)
    return pl.pallas_call(
        layer_kernel,
        out_shape=(
            jax.ShapeDtypeStruct((rows, width), bf16),
            jax.ShapeDtypeStruct((2, HALF, 4 * SUF), bf16),
        ),
        in_specs=[pl.BlockSpec(memory_space=pltpu.SMEM)] * len(scalars) + [vmem] * len(arrays),
        out_specs=[vmem] * 2,
        scratch_shapes=[
            pltpu.VMEM((8, 2, HD, kv_own.shape[2]), bf16),
            pltpu.VMEM((16, rows, width), bf16),
            pltpu.VMEM((8, 2, 192, 192), bf16),
            pltpu.VMEM((4, 2, 4, 2, 2, HD, 192), bf16),
            pltpu.VMEM((4, 2, 2, 3, 192, 256), bf16),
            pltpu.VMEM((192, 192), bf16),
            pltpu.VMEM((4, SUF, HD), bf16),
            pltpu.VMEM((4, HD, SUF), bf16),
            pltpu.VMEM((4, HD, SUF), bf16),
            pltpu.VMEM((4, HD, SUF), bf16),
            pltpu.VMEM((16, HD, 128), bf16),
            pltpu.VMEM((4, 2, rows, width), bf16),
            pltpu.VMEM((4, 2, rows, width), bf16),
            pltpu.VMEM((4, rows, width), bf16),
            pltpu.VMEM((4, rows, width), f32),
            pltpu.VMEM((2, 64, width), bf16),
            pltpu.VMEM((4, 64, width), bf16),
            pltpu.VMEM((4, 64, width), bf16),
            pltpu.VMEM((rows, width), bf16),
            pltpu.SemaphoreType.DMA((SEMS,)),
            pltpu.SemaphoreType.DMA((SEMS,)),
            pltpu.SemaphoreType.DMA((16,)),
            pltpu.SemaphoreType.DMA((16,)),
            pltpu.SemaphoreType.DMA((8,)),
        ],
        compiler_params=pltpu.CompilerParams(
            collective_id=0, has_side_effects=True, vmem_limit_bytes=67_043_328
        ),
        name="layer_kernel",
    )(*scalars, *arrays)


def local(
    tokens,
    attention_gain,
    feed_gain,
    w_query,
    w_key,
    w_value,
    w_out,
    w_gate,
    w_up,
    w_down,
    prefix_cache,
    lengths,
    member,
    owners,
):
    req, mdl = places()
    prefix_length = prefix_cache.shape[2]
    half = np.arange(HD // 2).astype(np.float32)
    frequency = np.float32(rope_base) ** (-(half * np.float32(2.0) / np.float32(HD)))
    positions = (np.arange(SUF) + prefix_length).astype(np.float32)
    angles = (frequency[:, None] * positions[None, :]).astype(np.float64)
    hidden, cache = layer(
        (lengths, member, owners),
        (
            prefix_cache[:, 0].transpose(0, 2, 1),
            tokens,
            w_query,
            w_key.T,
            w_value.T,
            w_out,
            w_gate,
            w_up,
            w_down.T,
            attention_gain[None, :],
            feed_gain[None, :],
            np.cos(angles).astype(np.float32),
            np.sin(angles).astype(np.float32),
        ),
    )
    own_offset = (mdl % 4) * tokens.shape[0] + jnp.arange(tokens.shape[0], dtype=jnp.int32)
    own_length = lax.dynamic_index_in_dim(lengths, req * 4 + mdl // 4, keepdims=False)
    own_valid = own_offset < own_length
    hidden = (hidden.astype(jnp.float32) * own_valid[:, None].astype(jnp.float32)).astype(
        jnp.bfloat16
    )
    return (hidden, cache.transpose(0, 2, 1))


def solution(mesh):
    placed = (
        P(("req", "mdl"), None),
        P(),
        P(),
        P("req", "mdl"),
        P("req", "mdl"),
        P("req", "mdl"),
        P("mdl", "req"),
        P("req", "mdl"),
        P("req", "mdl"),
        P("mdl", "req"),
        P(None, "req", None, "mdl"),
        P(),
        P(),
        P(),
    )
    return jax.shard_map(
        local,
        mesh=mesh,
        in_specs=placed,
        out_specs=(P(("req", "mdl"), None), P(None, "req", "mdl")),
        check_vma=False,
    )
```

```python
import math

import jax
import jax.numpy as jnp
import numpy as np
from jax import lax
from jax.experimental import pallas as pl
from jax.experimental.pallas import tpu as pltpu
from jax.sharding import PartitionSpec as P

HD = 96
HALF = 48
SUF = 512
rope_base = 100000.0
norm_eps = 1e-05
MESH = pl.DeviceIdType.MESH
LOG2E = 1.4426950408889634


def places():
    req = lax.axis_index("req")
    mdl = lax.axis_index("mdl")
    return req, mdl


class Hub:
    def __init__(self, send, recv):
        self.send, self.recv, self.made, self.pending = send, recv, [], []

    def copy(self, src, dst, device, awaited=True):
        index = len(self.made)
        made = pltpu.make_async_remote_copy(
            src_ref=src,
            dst_ref=dst,
            send_sem=self.send.at[index],
            recv_sem=self.recv.at[index],
            device_id=device,
            device_id_type=MESH,
        )
        made.start()
        self.made.append(made)
        if not awaited:
            self.pending.append(made)
        return made

    def shared(self):
        for made in self.pending:
            made.wait_recv()
        self.pending = []

    def finish(self):
        self.shared()
        for made in self.made:
            made.wait_send()


class Ring:
    def __init__(self, hub, region, piece, dev, u):
        self.hub, self.region, self.piece, self.dev = hub, region, piece, dev
        self.here, self.up_to, self.down_to, self.opposite = (
            u, lax.rem(u + 1, 4), lax.rem(u + 3, 4), lax.rem(u + 2, 4)
        )

    def start(self, src=None):
        block = self.region(self.here)
        src = block if src is None else src
        self.up = self.hub.copy(src, block, self.dev(self.up_to))
        self.down = self.hub.copy(src, block, self.dev(self.down_to))

    def near(self):
        self.up.wait_recv()
        self.down.wait_recv()

    def arrive(self, waited=False):
        if not waited:
            self.up.wait_recv()
        low = self.piece(self.down_to, 0)
        self.far_low = self.hub.copy(low, low, self.dev(self.up_to))
        if not waited:
            self.down.wait_recv()
        high = self.piece(self.up_to, 1)
        self.far_high = self.hub.copy(high, high, self.dev(self.down_to))

    def finish(self):
        self.far_low.wait_recv()
        self.far_high.wait_recv()

    def start_split(self, src=None):
        up, down = self.dev(self.up_to), self.dev(self.down_to)
        to = [self.piece(self.here, h) for h in range(2)]
        of = to if src is None else [src.at[h] for h in range(2)]
        self.up = self.hub.copy(of[0], to[0], up)
        self.down = self.hub.copy(of[1], to[1], down)
        self.up_rest = self.hub.copy(of[1], to[1], up)
        self.down_rest = self.hub.copy(of[0], to[0], down)

    def rest(self):
        self.up_rest.wait_recv()
        self.down_rest.wait_recv()

    def share(self, u, device, awaited=True):
        block = self.region(u)
        return self.hub.copy(block, block, device, awaited)


class Direct:
    def __init__(self, hub, region, dev, u):
        self.hub, self.region, self.dev, self.here = hub, region, dev, u

    def start(self, src=None):
        block = self.region(self.here)
        src = block if src is None else src
        self.sent = [
            self.hub.copy(src, block, self.dev(lax.rem(self.here + step, 4)))
            for step in (1, 3, 2)
        ]

    def finish(self):
        for made in self.sent:
            made.wait_recv()


class Spread:
    def __init__(self, hub, own, block, piece, u, v, dev, partner):
        self.hub, self.own, self.partner = hub, own, partner
        self.here, self.other = block(u, v), block(u, 1 - v)
        self.pair_dev = dev(u, 1 - v)
        self.handed = []

        def ring(w):
            return Ring(
                hub,
                lambda p: block(p, w),
                lambda p, h: piece(block(p, w), h),
                lambda p: dev(p, v),
                u,
            )

        self.rings = (ring(v), ring(1 - v))

    def start_pair(self):
        self.pair = self.hub.copy(self.own, self.here, self.pair_dev)

    def start_ring(self):
        self.rings[0].start(self.own)
        self.handed.append(self.hub.copy(self.own, self.here, self.partner))

    def pair_arrived(self):
        self.pair.wait_recv()
        self.rings[1].start()
        self.handed.append(self.hub.copy(self.other, self.other, self.partner))

    def ring_arrived(self, which):
        ring = self.rings[which]
        ring.arrive()
        self.hand(ring, ring.down_to)
        self.hand(ring, ring.up_to)

    def far_arrived(self, which):
        ring = self.rings[which]
        ring.finish()
        self.hand(ring, ring.opposite)

    def hand(self, ring, u):
        block = ring.region(u)
        self.handed.append(self.hub.copy(block, block, self.partner))

    def shared(self):
        for made in self.handed:
            made.wait_recv()


SEMS = 136
KV_EARLY = 3072


def layer_kernel(
    lengths, member, owners,
    kv_in, tok_in, wq_in, wk_in, wv_in, wo_in, wg_in, wu_in, wd_in,
    gain_ref, feed_gain_ref, cos_ref, sin_ref,
    out_ref, cache_ref,
    kv_all, tok_all, wqkv, wo, wm, pack, query, keys, values, att_out, att,
    rows_all, part, from_pair, sums, relay, plain, joined, to_relay,
    send, recv, a2a_send, a2a_recv, local_sem,
):
    req, mdl = places()
    x, yh = req // 2, lax.rem(req, 2)
    z, yl, core = mdl // 4, lax.rem(mdl // 2, 2), lax.rem(mdl, 2)
    y = yh * 2 + yl
    quarter = lax.rem(mdl, 4)
    width = tok_in.shape[1]
    partner = {"req": req, "mdl": z * 4 + yl * 2 + 1 - core}
    rows = pl.ds(pl.multiple_of(core * HALF, HALF), HALF)

    def kv_dev(u, v):
        return {"req": u * 2 + v, "mdl": mdl}

    def tok_dev(u, v):
        return {"req": req, "mdl": u * 4 + v * 2 + core}

    def x_dev(u):
        return kv_dev(u, yh)

    def y_dev(u):
        return {"req": x * 2 + u // 2, "mdl": z * 4 + lax.rem(u, 2) * 2 + core}

    def z_dev(u):
        return tok_dev(u, yl)

    barrier = pltpu.get_barrier_semaphore()
    peers = [kv_dev(x, 1 - yh)]
    peers += [x_dev(lax.rem(x + step, 4)) for step in (1, 2, 3)]
    peers += [y_dev(lax.rem(y + step, 4)) for step in (1, 3)]
    peers += [{"req": req, "mdl": lax.rem(mdl + step, 16)} for step in range(1, 16)]
    for peer in peers:
        pl.semaphore_signal(barrier, inc=1, device_id=peer, device_id_type=MESH)

    keep = []

    def store(src, dst):
        made = pltpu.make_async_copy(src, dst, local_sem.at[len(keep)])
        made.start()
        keep.append(made)

    store(wo_in, wo.at[z, core, x, yh, yl])
    for kind, ref in enumerate((wg_in, wu_in, wd_in)):
        store(ref, wm.at[x, yh, yl, kind])
    store(kv_in, kv_all.at[req, :, rows, :])
    store(tok_in, tok_all.at[mdl])
    pack[:, 0:HD] = wq_in[...]
    pack[:, HD : HD + HALF] = jnp.transpose(wk_in[...])
    pack[:, HD + HALF : 2 * HD] = jnp.transpose(wv_in[...])
    pl.semaphore_wait(barrier, len(peers))

    hub = Hub(send, recv)
    early, late = pl.ds(0, KV_EARLY), pl.ds(KV_EARLY, kv_all.shape[3] - KV_EARLY)
    kv_ring = Ring(
        hub,
        lambda u: kv_all.at[u * 2 + yh, :, rows],
        lambda u, h: kv_all.at[u * 2 + yh, h, rows],
        x_dev, x,
    )
    kv_other = Ring(
        hub,
        lambda u: kv_all.at[u * 2 + 1 - yh, :, rows, early],
        lambda u, h: kv_all.at[u * 2 + 1 - yh, h, rows, early],
        x_dev, x,
    )
    kv_pair = kv_dev(x, 1 - yh)
    handed = []

    def hand(block):
        handed.append(hub.copy(block, block, partner))

    def cross(u):
        block = kv_all.at[u * 2 + yh, :, rows, late]
        return hub.copy(block, block, kv_pair)

    def crossed(u, made):
        made.wait_recv()
        hand(kv_all.at[u * 2 + 1 - yh, :, rows, late])

    tok = Spread(
        hub, tok_in,
        lambda u, v: tok_all.at[u * 4 + v * 2 + core],
        lambda ref, h: ref.at[pl.ds(64 * h, 64)],
        z, yl, tok_dev, partner,
    )
    qkv = Spread(
        hub, pack,
        lambda u, v: wqkv.at[u * 2 + v, core],
        lambda ref, h: ref.at[pl.ds(96 * h, 96)],
        x, yh, kv_dev, partner,
    )
    wo_x = Direct(hub, lambda u: wo.at[z, core, u, yh, yl], x_dev, x)
    wo_y = Direct(hub, lambda u: wo.at[z, core, :, u // 2, lax.rem(u, 2)], y_dev, y)
    wo_z = Ring(
        hub,
        lambda u: wo.at[u, core],
        lambda u, h: wo.at[u, core, pl.ds(2 * h, 2)],
        z_dev, z,
    )
    wm_x = Ring(
        hub,
        lambda u: wm.at[u, yh, yl, 0:2],
        lambda u, h: wm.at[u, yh, yl, 0:2, pl.ds(96 * h, 96)],
        x_dev, x,
    )

    def wm_ring(step):
        u_x = lax.rem(x + step, 4)
        return Ring(
            hub,
            lambda u: wm.at[u_x, u // 2, lax.rem(u, 2), 0:2],
            lambda u, h: wm.at[u_x, u // 2, lax.rem(u, 2), 0:2, pl.ds(96 * h, 96)],
            y_dev, y,
        )

    wm_y = [wm_ring(step) for step in range(4)]
    wd_y = Ring(
        hub,
        lambda u: wm.at[x, u // 2, lax.rem(u, 2), 2],
        lambda u, h: wm.at[x, u // 2, lax.rem(u, 2), 2, pl.ds(96 * h, 96)],
        y_dev, y,
    )
    wd_x = Ring(
        hub,
        lambda u: wm.at[u, :, :, 2],
        lambda u, h: wm.at[u, h, :, 2],
        x_dev, x,
    )

    def project(r, carry):
        numbers = tok_all[pl.ds(4 * r, 4)].reshape(SUF, width).astype(jnp.float32)
        scale = lax.rsqrt(jnp.mean(numbers * numbers, axis=-1, keepdims=True) + norm_eps)
        normed = (numbers * scale * gain_ref[...].astype(jnp.float32)).astype(jnp.bfloat16)
        halves = [
            jnp.transpose(
                jnp.dot(
                    normed, wqkv[:, c].reshape(width, 192), preferred_element_type=jnp.float32
                )
            )
            for c in range(2)
        ]
        cosine, sine = cos_ref[...], sin_ref[...]

        def rotate(block):
            low, high = block[:HALF], block[HALF:]
            return jnp.concatenate(
                [low * cosine - high * sine, high * cosine + low * sine], axis=0
            )

        first = core == 0
        query_raw = jnp.where(first, halves[0][:HD], halves[1][:HD])
        keys_wide = rotate(jnp.concatenate([half[HD : HD + HALF] for half in halves], axis=0))
        values_wide = jnp.concatenate([half[HD + HALF :] for half in halves], axis=0)
        query[r] = jnp.transpose(rotate(query_raw)).astype(jnp.bfloat16)
        keys[r] = keys_wide.astype(jnp.bfloat16)
        values[r] = values_wide.astype(jnp.bfloat16)
        length = lengths[req * 4 + r]
        live = (lax.broadcasted_iota(jnp.int32, (HALF, SUF), 1) < length).astype(jnp.float32)
        columns = pl.ds(pl.multiple_of(r * SUF, SUF), SUF)
        for kind, wide in enumerate((keys_wide, values_wide)):
            own = jnp.where(first, wide[:HALF], wide[HALF:])
            cache_ref[kind, :, columns] = (own * live).astype(jnp.bfloat16)
        return carry

    def attend(i, carry):
        r = lax.rem(z + 1 + i, 4)
        length = lengths[req * 4 + r]
        slot = owners[member[req * 4 + r]]
        factor = LOG2E / math.sqrt(HD)
        chunk = 1024
        top = total = summed = None
        for j in range(0, kv_all.shape[3] + 1, chunk):
            own = j == kv_all.shape[3]
            if own:
                key_part, value_part = keys[r], values[r]
            else:
                key_part = kv_all[slot, 0, :, j : j + chunk]
                value_part = kv_all[slot, 1, :, j : j + chunk]
            scores = jnp.dot(query[r], key_part, preferred_element_type=jnp.float32)
            if own:
                row = lax.broadcasted_iota(jnp.int32, scores.shape, 0)
                column = lax.broadcasted_iota(jnp.int32, scores.shape, 1)
                allowed = (column <= row) & (column < length)
                scores = jnp.where(allowed, scores, -1e30)
            part_top = jnp.max(scores, axis=-1, keepdims=True)
            new_top = part_top if top is None else jnp.maximum(top, part_top)
            weights = jnp.exp2((scores - new_top) * factor)
            if own:
                weights = jnp.where(allowed, weights, 0.0)
            part_total = jnp.sum(weights, axis=-1, keepdims=True)
            part_sum = lax.dot_general(
                weights.astype(jnp.bfloat16),
                value_part,
                (((1,), (1,)), ((), ())),
                preferred_element_type=jnp.float32,
            )
            if top is None:
                total, summed = part_total, part_sum
            else:
                carried = jnp.exp2((top - new_top) * factor)
                total = total * carried + part_total
                summed = summed * carried + part_sum
            top = new_top
        att_out[r] = jnp.transpose(summed / total).astype(jnp.bfloat16)
        for j in range(4):

            @pl.when(r * 4 + j != mdl)
            def _():
                pltpu.make_async_remote_copy(
                    src_ref=att_out.at[r, :, pl.ds(128 * j, 128)],
                    dst_ref=att.at[mdl],
                    send_sem=a2a_send.at[i * 4 + j],
                    recv_sem=a2a_recv.at[i * 4 + quarter],
                    device_id={"req": req, "mdl": r * 4 + j},
                    device_id_type=MESH,
                ).start()

        return carry

    kv_here = kv_ring.region(x)
    wo_x.start(wo_in)
    tok.start_pair()
    kv_ring.start_split(kv_in)
    tok.start_ring()
    qkv.start_pair()
    kv_over = hub.copy(kv_in, kv_here, kv_pair)
    qkv.start_ring()
    handed.append(hub.copy(kv_in, kv_here, partner))
    store(pack, wqkv.at[req, core])
    keep[0].wait()
    wo_x.finish()
    wo_y.start()
    wd_y.start(wd_in)
    kv_ring.arrive()
    tok.pair_arrived()
    tok.ring_arrived(0)
    qkv.pair_arrived()
    for made in keep[1:4]:
        made.wait()
    wm_x.start()
    kv_ring.rest()
    cross_low = cross(kv_ring.down_to)
    cross_high = cross(kv_ring.up_to)
    hand(kv_ring.region(kv_ring.down_to))
    hand(kv_ring.region(kv_ring.up_to))
    qkv.ring_arrived(0)
    kv_over.wait_recv()
    kv_other.start_split()
    hand(kv_all.at[x * 2 + 1 - yh, :, rows])
    tok.ring_arrived(1)
    qkv.ring_arrived(1)
    kv_ring.finish()
    cross_far = cross(kv_ring.opposite)
    hand(kv_ring.region(kv_ring.opposite))
    wm_y[0].start()
    wo_y.finish()
    wo_z.start()
    wo_z.share(z, partner, False)
    wd_y.arrive()
    wm_x.near()
    wm_y[3].start()
    wm_y[1].start()
    tok.far_arrived(0)
    tok.far_arrived(1)
    qkv.far_arrived(0)
    kv_other.arrive()
    wm_x.arrive(True)
    wd_y.finish()
    wd_x.start()
    qkv.far_arrived(1)
    for made in keep[4:]:
        made.wait()
    tok.shared()
    qkv.shared()
    lax.fori_loop(0, 4, project, 0)
    crossed(kv_ring.down_to, cross_low)
    crossed(kv_ring.up_to, cross_high)
    kv_other.rest()
    hand(kv_other.region(kv_other.down_to))
    hand(kv_other.region(kv_other.up_to))
    crossed(kv_ring.opposite, cross_far)
    kv_other.finish()
    hand(kv_other.region(kv_other.opposite))
    for made in handed:
        made.wait_recv()
    wm_y[0].arrive()
    wo_z.arrive()
    wo_z.share(wo_z.down_to, partner, False)
    wo_z.share(wo_z.up_to, partner, False)
    attend(0, 0)
    wm_x.finish()
    wm_y[2].start()
    wd_x.arrive()
    attend(1, 0)
    wo_z.finish()
    wo_z.share(wo_z.opposite, partner, False)
    wm_y[3].arrive()
    wm_y[1].arrive()
    attend(2, 0)
    attend(3, 0)
    wm_y[2].arrive()
    att[mdl] = att_out[z, :, pl.ds(pl.multiple_of(quarter * 128, 128), 128)]

    def exchange(i, j, sending):
        k = i * 4 + j
        made = pltpu.make_async_remote_copy(
            src_ref=att_out.at[0, :, pl.ds(0, 128)],
            dst_ref=att.at[j],
            send_sem=a2a_send.at[k],
            recv_sem=a2a_recv.at[k],
            device_id=partner,
            device_id_type=MESH,
        )

        def wait():
            made.wait_send() if sending else made.wait_recv()

        if i < 3:
            wait()
        else:
            pl.when(quarter != j)(wait)

    hub.shared()
    for i in range(4):
        for j in range(4):
            exchange(i, j, False)
    attended = jnp.transpose(att[...].reshape(16 * HD, 128))
    own_rows = rows_all.at[z, core]
    for u in range(4):
        attention = jnp.concatenate(
            [
                jnp.dot(
                    attended,
                    jnp.concatenate(
                        [wo[k // 4, k % 2, u, v, (k // 2) % 2] for k in range(16)], axis=0
                    ),
                    preferred_element_type=jnp.float32,
                )
                for v in range(2)
            ],
            axis=1,
        )
        here = slice(384 * u, 384 * u + 384)
        own_rows[:, here] = (tok_all[mdl, :, here].astype(jnp.float32) + attention).astype(jnp.bfloat16)

    def peer(du, flip=False):
        other = 1 - core if flip else core
        return {"req": req, "mdl": lax.rem(z + du, 4) * 4 + yl * 2 + other}

    go = hub.copy
    gathered = Ring(
        hub,
        lambda u: rows_all.at[u, core],
        lambda u, h: rows_all.at[u, core, pl.ds(64 * h, 64)],
        z_dev, z,
    )
    gathered.start_split()
    across = go(own_rows, own_rows, partner)
    for ring in wm_y + [wd_x]:
        ring.finish()

    def feed(slot, du):
        there = rows_all.at[lax.rem(z + du, 4)]
        numbers = there[...].reshape(256, width).astype(jnp.float32)
        scale = lax.rsqrt(jnp.mean(numbers * numbers, axis=-1, keepdims=True) + norm_eps)
        normed = (numbers * scale * feed_gain_ref[...].astype(jnp.float32)).astype(jnp.bfloat16)
        active = []
        for block in range(2):
            gate = jnp.dot(
                normed,
                wm[:, :, block, 0].reshape(width, 256),
                preferred_element_type=jnp.float32,
            )
            lift = jnp.dot(
                normed,
                wm[:, :, block, 1].reshape(width, 256),
                preferred_element_type=jnp.float32,
            )
            active.append((gate / (1.0 + jnp.exp(-gate)) * lift).astype(jnp.bfloat16))
        for u in range(4):
            parts = [
                lax.dot_general(
                    active[block],
                    wm[u, :, block, 2].reshape(384, 256),
                    (((1,), (1,)), ((), ())),
                    preferred_element_type=jnp.float32,
                )
                for block in range(2)
            ]
            part[slot, :, :, 384 * u : 384 * u + 384] = (
                (parts[0] + parts[1]).astype(jnp.bfloat16).reshape(2, 128, 384)
            )
        return go(part.at[slot, 1 - core], from_pair.at[slot], peer(0, True))

    def pair_sum(slot, copy):
        copy.wait_recv()
        sums[slot] = part[slot, core].astype(jnp.float32) + from_pair[slot].astype(jnp.float32)

    across.wait_recv()
    pair0 = feed(0, 0)
    gathered.arrive()
    gathered.up_rest.wait_recv()
    low_p = gathered.share(gathered.down_to, partner)
    gathered.down_rest.wait_recv()
    high_p = gathered.share(gathered.up_to, partner)
    low_p.wait_recv()
    pair3 = feed(3, 3)
    gathered.finish()
    far_p = gathered.share(gathered.opposite, partner)
    pair_sum(3, pair3)
    plain[0] = sums[3, 0:64].astype(jnp.bfloat16)
    plain_a = go(plain.at[0], plain.at[2], peer(3))
    far_p.wait_recv()
    pair2 = feed(2, 2)
    high_p.wait_recv()
    pair_sum(2, pair2)
    to_relay[...] = sums[2].astype(jnp.bfloat16)
    relay_a = go(to_relay.at[pl.ds(0, 64)], relay.at[0], peer(1))
    relay_b = go(to_relay.at[pl.ds(64, 64)], relay.at[1], peer(3))
    pair1 = feed(1, 1)
    pair_sum(1, pair1)
    plain[1] = sums[1, 64:128].astype(jnp.bfloat16)
    plain_b = go(plain.at[1], plain.at[3], peer(1))
    pair_sum(0, pair0)
    relay_a.wait_recv()
    joined[0] = (sums[1, 0:64] + relay[0].astype(jnp.float32)).astype(jnp.bfloat16)
    joined_a = go(joined.at[0], joined.at[2], peer(1))
    relay_b.wait_recv()
    joined[1] = (sums[3, 64:128] + relay[1].astype(jnp.float32)).astype(jnp.bfloat16)
    joined_b = go(joined.at[1], joined.at[3], peer(3))
    plain_a.wait_recv()
    plain_b.wait_recv()
    joined_a.wait_recv()
    joined_b.wait_recv()
    for h in range(2):
        here = slice(64 * h, 64 * h + 64)
        feed_sum = (
            sums[0, here]
            + plain[2 + h].astype(jnp.float32)
            + joined[2 + h].astype(jnp.float32)
        )
        place = quarter * 128 + 64 * h + lax.broadcasted_iota(jnp.int32, (64, 1), 0)
        live = (place < lengths[req * 4 + z]).astype(jnp.float32)
        out_ref[here, :] = (
            (own_rows[here, :].astype(jnp.float32) + feed_sum) * live
        ).astype(jnp.bfloat16)
    for i in range(4):
        for j in range(4):
            exchange(i, j, True)
    hub.finish()


def layer(scalars, arrays):
    kv_own, tokens = arrays[:2]
    rows, width = tokens.shape
    bf16, f32 = jnp.bfloat16, jnp.float32
    vmem = pl.BlockSpec(memory_space=pltpu.VMEM)
    hbm = pl.BlockSpec(memory_space=pl.ANY)
    return pl.pallas_call(
        layer_kernel,
        out_shape=(
            jax.ShapeDtypeStruct((rows, width), bf16),
            jax.ShapeDtypeStruct((2, HALF, 4 * SUF), bf16),
        ),
        in_specs=[pl.BlockSpec(memory_space=pltpu.SMEM)] * len(scalars)
        + [hbm, hbm, vmem, vmem, vmem, hbm, hbm, hbm, hbm, vmem, vmem, vmem, vmem],
        out_specs=[vmem] * 2,
        scratch_shapes=[
            pltpu.VMEM((8, 2, HD, kv_own.shape[2]), bf16),
            pltpu.VMEM((16, rows, width), bf16),
            pltpu.VMEM((8, 2, 192, 192), bf16),
            pltpu.VMEM((4, 2, 4, 2, 2, HD, 192), bf16),
            pltpu.VMEM((4, 2, 2, 3, 192, 256), bf16),
            pltpu.VMEM((192, 192), bf16),
            pltpu.VMEM((4, SUF, HD), bf16),
            pltpu.VMEM((4, HD, SUF), bf16),
            pltpu.VMEM((4, HD, SUF), bf16),
            pltpu.VMEM((4, HD, SUF), bf16),
            pltpu.VMEM((16, HD, 128), bf16),
            pltpu.VMEM((4, 2, rows, width), bf16),
            pltpu.VMEM((4, 2, rows, width), bf16),
            pltpu.VMEM((4, rows, width), bf16),
            pltpu.VMEM((4, rows, width), f32),
            pltpu.VMEM((2, 64, width), bf16),
            pltpu.VMEM((4, 64, width), bf16),
            pltpu.VMEM((4, 64, width), bf16),
            pltpu.VMEM((rows, width), bf16),
            pltpu.SemaphoreType.DMA((SEMS,)),
            pltpu.SemaphoreType.DMA((SEMS,)),
            pltpu.SemaphoreType.DMA((16,)),
            pltpu.SemaphoreType.DMA((16,)),
            pltpu.SemaphoreType.DMA((8,)),
        ],
        compiler_params=pltpu.CompilerParams(
            collective_id=0, has_side_effects=True, vmem_limit_bytes=67_043_328
        ),
        name="layer_kernel",
    )(*scalars, *arrays)


def local(
    tokens,
    attention_gain,
    feed_gain,
    w_query,
    w_key,
    w_value,
    w_out,
    w_gate,
    w_up,
    w_down,
    prefix_cache,
    lengths,
    member,
    owners,
):
    prefix_length = prefix_cache.shape[2]
    half = np.arange(HD // 2).astype(np.float32)
    frequency = np.float32(rope_base) ** (-(half * np.float32(2.0) / np.float32(HD)))
    positions = (np.arange(SUF) + prefix_length).astype(np.float32)
    angles = (frequency[:, None] * positions[None, :]).astype(np.float64)
    hidden, cache = layer(
        (lengths, member, owners),
        (
            prefix_cache[:, 0].transpose(0, 2, 1),
            tokens,
            w_query,
            w_key.T,
            w_value.T,
            w_out,
            w_gate,
            w_up,
            w_down.T,
            attention_gain[None, :],
            feed_gain[None, :],
            np.cos(angles).astype(np.float32),
            np.sin(angles).astype(np.float32),
        ),
    )
    return (hidden, cache.transpose(0, 2, 1))


def solution(mesh):
    placed = (
        P(("req", "mdl"), None),
        P(),
        P(),
        P("req", "mdl"),
        P("req", "mdl"),
        P("req", "mdl"),
        P("mdl", "req"),
        P("req", "mdl"),
        P("req", "mdl"),
        P("mdl", "req"),
        P(None, "req", None, "mdl"),
        P(),
        P(),
        P(),
    )
    return jax.shard_map(
        local,
        mesh=mesh,
        in_specs=placed,
        out_specs=(P(("req", "mdl"), None), P(None, "req", "mdl")),
        check_vma=False,
    )
```

```python
import math

import jax
import jax.numpy as jnp
import numpy as np
from jax import lax
from jax.experimental import pallas as pl
from jax.experimental.pallas import tpu as pltpu
from jax.sharding import PartitionSpec as P

HD = 96
HALF = 48
SUF = 512
rope_base = 100000.0
norm_eps = 1e-05
MESH = pl.DeviceIdType.MESH
LOG2E = 1.4426950408889634


def places():
    req = lax.axis_index("req")
    mdl = lax.axis_index("mdl")
    return req, mdl


class Hub:
    def __init__(self, send, recv):
        self.send, self.recv, self.made, self.pending = send, recv, [], []

    def copy(self, src, dst, device, awaited=True):
        index = len(self.made)
        made = pltpu.make_async_remote_copy(
            src_ref=src,
            dst_ref=dst,
            send_sem=self.send.at[index],
            recv_sem=self.recv.at[index],
            device_id=device,
            device_id_type=MESH,
        )
        made.start()
        self.made.append(made)
        if not awaited:
            self.pending.append(made)
        return made

    def shared(self):
        for made in self.pending:
            made.wait_recv()
        self.pending = []

    def finish(self):
        self.shared()
        for made in self.made:
            made.wait_send()


class Ring:
    def __init__(self, hub, region, piece, dev, u):
        self.hub, self.region, self.piece, self.dev = hub, region, piece, dev
        self.here, self.up_to, self.down_to, self.opposite = (
            u, lax.rem(u + 1, 4), lax.rem(u + 3, 4), lax.rem(u + 2, 4)
        )

    def start(self, src=None):
        block = self.region(self.here)
        src = block if src is None else src
        self.up = self.hub.copy(src, block, self.dev(self.up_to))
        self.down = self.hub.copy(src, block, self.dev(self.down_to))

    def near(self):
        self.up.wait_recv()
        self.down.wait_recv()

    def arrive(self, waited=False):
        if not waited:
            self.up.wait_recv()
        low = self.piece(self.down_to, 0)
        self.far_low = self.hub.copy(low, low, self.dev(self.up_to))
        if not waited:
            self.down.wait_recv()
        high = self.piece(self.up_to, 1)
        self.far_high = self.hub.copy(high, high, self.dev(self.down_to))

    def finish(self):
        self.far_low.wait_recv()
        self.far_high.wait_recv()

    def start_split(self, src=None):
        up, down = self.dev(self.up_to), self.dev(self.down_to)
        to = [self.piece(self.here, h) for h in range(2)]
        of = to if src is None else [src.at[h] for h in range(2)]
        self.up = self.hub.copy(of[0], to[0], up)
        self.down = self.hub.copy(of[1], to[1], down)
        self.up_rest = self.hub.copy(of[1], to[1], up)
        self.down_rest = self.hub.copy(of[0], to[0], down)

    def rest(self):
        self.up_rest.wait_recv()
        self.down_rest.wait_recv()

    def share(self, u, device, awaited=True):
        block = self.region(u)
        return self.hub.copy(block, block, device, awaited)


class Direct:
    def __init__(self, hub, region, dev, u):
        self.hub, self.region, self.dev, self.here = hub, region, dev, u

    def start(self, src=None):
        block = self.region(self.here)
        src = block if src is None else src
        self.sent = [
            self.hub.copy(src, block, self.dev(lax.rem(self.here + step, 4)))
            for step in (1, 3, 2)
        ]

    def finish(self):
        for made in self.sent:
            made.wait_recv()


class Spread:
    def __init__(self, hub, own, block, piece, u, v, dev, partner):
        self.hub, self.own, self.partner = hub, own, partner
        self.here, self.other = block(u, v), block(u, 1 - v)
        self.pair_dev = dev(u, 1 - v)
        self.handed = []

        def ring(w):
            return Ring(
                hub,
                lambda p: block(p, w),
                lambda p, h: piece(block(p, w), h),
                lambda p: dev(p, v),
                u,
            )

        self.rings = (ring(v), ring(1 - v))

    def start_pair(self):
        self.pair = self.hub.copy(self.own, self.here, self.pair_dev)

    def start_ring(self):
        self.rings[0].start(self.own)
        self.handed.append(self.hub.copy(self.own, self.here, self.partner))

    def pair_arrived(self):
        self.pair.wait_recv()
        self.rings[1].start()
        self.handed.append(self.hub.copy(self.other, self.other, self.partner))

    def ring_arrived(self, which):
        ring = self.rings[which]
        ring.arrive()
        self.hand(ring, ring.down_to)
        self.hand(ring, ring.up_to)

    def far_arrived(self, which):
        ring = self.rings[which]
        ring.finish()
        self.hand(ring, ring.opposite)

    def hand(self, ring, u):
        block = ring.region(u)
        self.handed.append(self.hub.copy(block, block, self.partner))

    def shared(self):
        for made in self.handed:
            made.wait_recv()


SEMS = 136
KV_EARLY = 3072


def layer_kernel(
    lengths, member, owners,
    kv_in, tok_in, wq_in, wk_in, wv_in, wo_in, wg_in, wu_in, wd_in,
    gain_ref, feed_gain_ref, cos_ref, sin_ref,
    out_ref, cache_ref,
    kv_all, tok_all, wqkv, wo, wm, pack, query, keys, values, att_out, att,
    rows_all, part, from_pair, sums, relay, plain, joined, to_relay,
    send, recv, a2a_send, a2a_recv, local_sem,
):
    req, mdl = places()
    x, yh = req // 2, lax.rem(req, 2)
    z, yl, core = mdl // 4, lax.rem(mdl // 2, 2), lax.rem(mdl, 2)
    y = yh * 2 + yl
    quarter = lax.rem(mdl, 4)
    width = tok_in.shape[1]
    partner = {"req": req, "mdl": z * 4 + yl * 2 + 1 - core}
    rows = pl.ds(pl.multiple_of(core * HALF, HALF), HALF)

    def kv_dev(u, v):
        return {"req": u * 2 + v, "mdl": mdl}

    def tok_dev(u, v):
        return {"req": req, "mdl": u * 4 + v * 2 + core}

    def x_dev(u):
        return kv_dev(u, yh)

    def y_dev(u):
        return {"req": x * 2 + u // 2, "mdl": z * 4 + lax.rem(u, 2) * 2 + core}

    def z_dev(u):
        return tok_dev(u, yl)

    barrier = pltpu.get_barrier_semaphore()
    peers = [kv_dev(x, 1 - yh)]
    peers += [x_dev(lax.rem(x + step, 4)) for step in (1, 2, 3)]
    peers += [y_dev(lax.rem(y + step, 4)) for step in (1, 3)]
    peers += [{"req": req, "mdl": lax.rem(mdl + step, 16)} for step in range(1, 16)]
    for peer in peers:
        pl.semaphore_signal(barrier, inc=1, device_id=peer, device_id_type=MESH)

    keep = []

    def store(src, dst):
        made = pltpu.make_async_copy(src, dst, local_sem.at[len(keep)])
        made.start()
        keep.append(made)

    store(wo_in, wo.at[z, core, x, yh, yl])
    for kind, ref in enumerate((wg_in, wu_in, wd_in)):
        store(ref, wm.at[x, yh, yl, kind])
    store(kv_in, kv_all.at[req, :, rows, :])
    store(tok_in, tok_all.at[mdl])
    pack[:, 0:HD] = wq_in[...]
    pack[:, HD : HD + HALF] = jnp.transpose(wk_in[...])
    pack[:, HD + HALF : 2 * HD] = jnp.transpose(wv_in[...])
    pl.semaphore_wait(barrier, len(peers))

    hub = Hub(send, recv)
    early, late = pl.ds(0, KV_EARLY), pl.ds(KV_EARLY, kv_all.shape[3] - KV_EARLY)
    kv_ring = Ring(
        hub,
        lambda u: kv_all.at[u * 2 + yh, :, rows],
        lambda u, h: kv_all.at[u * 2 + yh, h, rows],
        x_dev, x,
    )
    kv_other = Ring(
        hub,
        lambda u: kv_all.at[u * 2 + 1 - yh, :, rows, early],
        lambda u, h: kv_all.at[u * 2 + 1 - yh, h, rows, early],
        x_dev, x,
    )
    kv_pair = kv_dev(x, 1 - yh)
    handed = []

    def hand(block):
        handed.append(hub.copy(block, block, partner))

    def cross(u):
        block = kv_all.at[u * 2 + yh, :, rows, late]
        return hub.copy(block, block, kv_pair)

    def crossed(u, made):
        made.wait_recv()
        hand(kv_all.at[u * 2 + 1 - yh, :, rows, late])

    tok = Spread(
        hub, tok_in,
        lambda u, v: tok_all.at[u * 4 + v * 2 + core],
        lambda ref, h: ref.at[pl.ds(64 * h, 64)],
        z, yl, tok_dev, partner,
    )
    qkv = Spread(
        hub, pack,
        lambda u, v: wqkv.at[u * 2 + v, core],
        lambda ref, h: ref.at[pl.ds(96 * h, 96)],
        x, yh, kv_dev, partner,
    )
    wo_x = Direct(hub, lambda u: wo.at[z, core, u, yh, yl], x_dev, x)
    wo_y = Direct(hub, lambda u: wo.at[z, core, :, u // 2, lax.rem(u, 2)], y_dev, y)
    wo_z = Ring(
        hub,
        lambda u: wo.at[u, core],
        lambda u, h: wo.at[u, core, pl.ds(2 * h, 2)],
        z_dev, z,
    )
    wm_x = Ring(
        hub,
        lambda u: wm.at[u, yh, yl],
        lambda u, h: wm.at[u, yh, yl, :, pl.ds(96 * h, 96)],
        x_dev, x,
    )

    def wm_ring(step):
        u_x = lax.rem(x + step, 4)
        return Ring(
            hub,
            lambda u: wm.at[u_x, u // 2, lax.rem(u, 2)],
            lambda u, h: wm.at[u_x, u // 2, lax.rem(u, 2), :, pl.ds(96 * h, 96)],
            y_dev, y,
        )

    wm_y = [wm_ring(step) for step in range(4)]

    def project(r, carry):
        numbers = tok_all[pl.ds(4 * r, 4)].reshape(SUF, width).astype(jnp.float32)
        scale = lax.rsqrt(jnp.mean(numbers * numbers, axis=-1, keepdims=True) + norm_eps)
        normed = (numbers * scale * gain_ref[...].astype(jnp.float32)).astype(jnp.bfloat16)
        halves = [
            jnp.transpose(
                jnp.dot(
                    normed, wqkv[:, c].reshape(width, 192), preferred_element_type=jnp.float32
                )
            )
            for c in range(2)
        ]
        cosine, sine = cos_ref[...], sin_ref[...]

        def rotate(block):
            low, high = block[:HALF], block[HALF:]
            return jnp.concatenate(
                [low * cosine - high * sine, high * cosine + low * sine], axis=0
            )

        first = core == 0
        query_raw = jnp.where(first, halves[0][:HD], halves[1][:HD])
        keys_wide = rotate(jnp.concatenate([half[HD : HD + HALF] for half in halves], axis=0))
        values_wide = jnp.concatenate([half[HD + HALF :] for half in halves], axis=0)
        query[r] = jnp.transpose(rotate(query_raw)).astype(jnp.bfloat16)
        keys[r] = keys_wide.astype(jnp.bfloat16)
        values[r] = values_wide.astype(jnp.bfloat16)
        length = lengths[req * 4 + r]
        live = (lax.broadcasted_iota(jnp.int32, (HALF, SUF), 1) < length).astype(jnp.float32)
        columns = pl.ds(pl.multiple_of(r * SUF, SUF), SUF)
        for kind, wide in enumerate((keys_wide, values_wide)):
            own = jnp.where(first, wide[:HALF], wide[HALF:])
            cache_ref[kind, :, columns] = (own * live).astype(jnp.bfloat16)
        return carry

    def attend(i, carry):
        r = lax.rem(z + 1 + i, 4)
        length = lengths[req * 4 + r]
        slot = owners[member[req * 4 + r]]
        factor = LOG2E / math.sqrt(HD)
        chunk = 1024
        top = total = summed = None
        for j in range(0, kv_all.shape[3] + 1, chunk):
            own = j == kv_all.shape[3]
            if own:
                key_part, value_part = keys[r], values[r]
            else:
                key_part = kv_all[slot, 0, :, j : j + chunk]
                value_part = kv_all[slot, 1, :, j : j + chunk]
            scores = jnp.dot(query[r], key_part, preferred_element_type=jnp.float32)
            if own:
                row = lax.broadcasted_iota(jnp.int32, scores.shape, 0)
                column = lax.broadcasted_iota(jnp.int32, scores.shape, 1)
                allowed = (column <= row) & (column < length)
                scores = jnp.where(allowed, scores, -1e30)
            part_top = jnp.max(scores, axis=-1, keepdims=True)
            new_top = part_top if top is None else jnp.maximum(top, part_top)
            weights = jnp.exp2((scores - new_top) * factor)
            if own:
                weights = jnp.where(allowed, weights, 0.0)
            part_total = jnp.sum(weights, axis=-1, keepdims=True)
            part_sum = lax.dot_general(
                weights.astype(jnp.bfloat16),
                value_part,
                (((1,), (1,)), ((), ())),
                preferred_element_type=jnp.float32,
            )
            if top is None:
                total, summed = part_total, part_sum
            else:
                carried = jnp.exp2((top - new_top) * factor)
                total = total * carried + part_total
                summed = summed * carried + part_sum
            top = new_top
        att_out[r] = jnp.transpose(summed / total).astype(jnp.bfloat16)
        for j in range(4):

            @pl.when(r * 4 + j != mdl)
            def _():
                pltpu.make_async_remote_copy(
                    src_ref=att_out.at[r, :, pl.ds(128 * j, 128)],
                    dst_ref=att.at[mdl],
                    send_sem=a2a_send.at[i * 4 + j],
                    recv_sem=a2a_recv.at[i * 4 + quarter],
                    device_id={"req": req, "mdl": r * 4 + j},
                    device_id_type=MESH,
                ).start()

        return carry

    kv_here = kv_ring.region(x)
    wo_x.start(wo_in)
    tok.start_pair()
    kv_ring.start_split(kv_in)
    tok.start_ring()
    qkv.start_pair()
    kv_over = hub.copy(kv_in, kv_here, kv_pair)
    qkv.start_ring()
    handed.append(hub.copy(kv_in, kv_here, partner))
    store(pack, wqkv.at[req, core])
    keep[0].wait()
    wo_x.finish()
    wo_y.start()
    kv_ring.arrive()
    tok.pair_arrived()
    tok.ring_arrived(0)
    qkv.pair_arrived()
    for made in keep[1:4]:
        made.wait()
    wm_x.start()
    kv_ring.rest()
    cross_low = cross(kv_ring.down_to)
    cross_high = cross(kv_ring.up_to)
    hand(kv_ring.region(kv_ring.down_to))
    hand(kv_ring.region(kv_ring.up_to))
    qkv.ring_arrived(0)
    kv_over.wait_recv()
    kv_other.start_split()
    hand(kv_all.at[x * 2 + 1 - yh, :, rows])
    tok.ring_arrived(1)
    qkv.ring_arrived(1)
    kv_ring.finish()
    cross_far = cross(kv_ring.opposite)
    hand(kv_ring.region(kv_ring.opposite))
    wm_y[0].start()
    wo_y.finish()
    wo_z.start()
    wo_z.share(z, partner, False)
    wm_x.near()
    wm_y[3].start()
    wm_y[1].start()
    tok.far_arrived(0)
    tok.far_arrived(1)
    qkv.far_arrived(0)
    kv_other.arrive()
    wm_x.arrive(True)
    qkv.far_arrived(1)
    for made in keep[4:]:
        made.wait()
    tok.shared()
    qkv.shared()
    lax.fori_loop(0, 4, project, 0)
    crossed(kv_ring.down_to, cross_low)
    crossed(kv_ring.up_to, cross_high)
    kv_other.rest()
    hand(kv_other.region(kv_other.down_to))
    hand(kv_other.region(kv_other.up_to))
    crossed(kv_ring.opposite, cross_far)
    kv_other.finish()
    hand(kv_other.region(kv_other.opposite))
    for made in handed:
        made.wait_recv()
    wm_y[0].arrive()
    wo_z.arrive()
    wo_z.share(wo_z.down_to, partner, False)
    wo_z.share(wo_z.up_to, partner, False)
    attend(0, 0)
    wm_x.finish()
    wm_y[2].start()
    attend(1, 0)
    wo_z.finish()
    wo_z.share(wo_z.opposite, partner, False)
    wm_y[3].arrive()
    wm_y[1].arrive()
    attend(2, 0)
    attend(3, 0)
    wm_y[2].arrive()
    att[mdl] = att_out[z, :, pl.ds(pl.multiple_of(quarter * 128, 128), 128)]

    def exchange(i, j, sending):
        k = i * 4 + j
        made = pltpu.make_async_remote_copy(
            src_ref=att_out.at[0, :, pl.ds(0, 128)],
            dst_ref=att.at[j],
            send_sem=a2a_send.at[k],
            recv_sem=a2a_recv.at[k],
            device_id=partner,
            device_id_type=MESH,
        )

        def wait():
            made.wait_send() if sending else made.wait_recv()

        if i < 3:
            wait()
        else:
            pl.when(quarter != j)(wait)

    hub.shared()
    for i in range(4):
        for j in range(4):
            exchange(i, j, False)
    attended = jnp.transpose(att[...].reshape(16 * HD, 128))
    own_rows = rows_all.at[z, core]
    for u in range(4):
        attention = jnp.concatenate(
            [
                jnp.dot(
                    attended,
                    jnp.concatenate(
                        [wo[k // 4, k % 2, u, v, (k // 2) % 2] for k in range(16)], axis=0
                    ),
                    preferred_element_type=jnp.float32,
                )
                for v in range(2)
            ],
            axis=1,
        )
        here = slice(384 * u, 384 * u + 384)
        own_rows[:, here] = (tok_all[mdl, :, here].astype(jnp.float32) + attention).astype(jnp.bfloat16)

    def peer(du, flip=False):
        other = 1 - core if flip else core
        return {"req": req, "mdl": lax.rem(z + du, 4) * 4 + yl * 2 + other}

    go = hub.copy
    gathered = Ring(
        hub,
        lambda u: rows_all.at[u, core],
        lambda u, h: rows_all.at[u, core, pl.ds(64 * h, 64)],
        z_dev, z,
    )
    gathered.start_split()
    across = go(own_rows, own_rows, partner)
    for ring in wm_y:
        ring.finish()

    def feed(slot, du):
        there = rows_all.at[lax.rem(z + du, 4)]
        numbers = there[...].reshape(256, width).astype(jnp.float32)
        scale = lax.rsqrt(jnp.mean(numbers * numbers, axis=-1, keepdims=True) + norm_eps)
        normed = (numbers * scale * feed_gain_ref[...].astype(jnp.float32)).astype(jnp.bfloat16)
        active = []
        for block in range(2):
            gate = jnp.dot(
                normed,
                wm[:, :, block, 0].reshape(width, 256),
                preferred_element_type=jnp.float32,
            )
            lift = jnp.dot(
                normed,
                wm[:, :, block, 1].reshape(width, 256),
                preferred_element_type=jnp.float32,
            )
            active.append((gate / (1.0 + jnp.exp(-gate)) * lift).astype(jnp.bfloat16))
        for u in range(4):
            parts = [
                lax.dot_general(
                    active[block],
                    wm[u, :, block, 2].reshape(384, 256),
                    (((1,), (1,)), ((), ())),
                    preferred_element_type=jnp.float32,
                )
                for block in range(2)
            ]
            part[slot, :, :, 384 * u : 384 * u + 384] = (
                (parts[0] + parts[1]).astype(jnp.bfloat16).reshape(2, 128, 384)
            )
        return go(part.at[slot, 1 - core], from_pair.at[slot], peer(0, True))

    def pair_sum(slot, copy):
        copy.wait_recv()
        sums[slot] = part[slot, core].astype(jnp.float32) + from_pair[slot].astype(jnp.float32)

    across.wait_recv()
    pair0 = feed(0, 0)
    gathered.arrive()
    gathered.up_rest.wait_recv()
    low_p = gathered.share(gathered.down_to, partner)
    gathered.down_rest.wait_recv()
    high_p = gathered.share(gathered.up_to, partner)
    low_p.wait_recv()
    pair3 = feed(3, 3)
    gathered.finish()
    far_p = gathered.share(gathered.opposite, partner)
    high_p.wait_recv()
    pair1 = feed(1, 1)
    pair_sum(3, pair3)
    plain[0] = sums[3, 0:64].astype(jnp.bfloat16)
    plain_a = go(plain.at[0], plain.at[2], peer(3))
    far_p.wait_recv()
    pair2 = feed(2, 2)
    pair_sum(1, pair1)
    plain[1] = sums[1, 64:128].astype(jnp.bfloat16)
    plain_b = go(plain.at[1], plain.at[3], peer(1))
    pair_sum(2, pair2)
    to_relay[...] = sums[2].astype(jnp.bfloat16)
    relay_a = go(to_relay.at[pl.ds(0, 64)], relay.at[0], peer(1))
    relay_b = go(to_relay.at[pl.ds(64, 64)], relay.at[1], peer(3))
    pair_sum(0, pair0)
    relay_a.wait_recv()
    joined[0] = (sums[1, 0:64] + relay[0].astype(jnp.float32)).astype(jnp.bfloat16)
    joined_a = go(joined.at[0], joined.at[2], peer(1))
    relay_b.wait_recv()
    joined[1] = (sums[3, 64:128] + relay[1].astype(jnp.float32)).astype(jnp.bfloat16)
    joined_b = go(joined.at[1], joined.at[3], peer(3))
    plain_a.wait_recv()
    plain_b.wait_recv()
    joined_a.wait_recv()
    joined_b.wait_recv()
    for h in range(2):
        here = slice(64 * h, 64 * h + 64)
        feed_sum = (
            sums[0, here]
            + plain[2 + h].astype(jnp.float32)
            + joined[2 + h].astype(jnp.float32)
        )
        place = quarter * 128 + 64 * h + lax.broadcasted_iota(jnp.int32, (64, 1), 0)
        live = (place < lengths[req * 4 + z]).astype(jnp.float32)
        out_ref[here, :] = (
            (own_rows[here, :].astype(jnp.float32) + feed_sum) * live
        ).astype(jnp.bfloat16)
    for i in range(4):
        for j in range(4):
            exchange(i, j, True)
    hub.finish()


def layer(scalars, arrays):
    kv_own, tokens = arrays[:2]
    rows, width = tokens.shape
    bf16, f32 = jnp.bfloat16, jnp.float32
    vmem = pl.BlockSpec(memory_space=pltpu.VMEM)
    hbm = pl.BlockSpec(memory_space=pl.ANY)
    return pl.pallas_call(
        layer_kernel,
        out_shape=(
            jax.ShapeDtypeStruct((rows, width), bf16),
            jax.ShapeDtypeStruct((2, HALF, 4 * SUF), bf16),
        ),
        in_specs=[pl.BlockSpec(memory_space=pltpu.SMEM)] * len(scalars)
        + [hbm, hbm, vmem, vmem, vmem, hbm, hbm, hbm, hbm, vmem, vmem, vmem, vmem],
        out_specs=[vmem] * 2,
        scratch_shapes=[
            pltpu.VMEM((8, 2, HD, kv_own.shape[2]), bf16),
            pltpu.VMEM((16, rows, width), bf16),
            pltpu.VMEM((8, 2, 192, 192), bf16),
            pltpu.VMEM((4, 2, 4, 2, 2, HD, 192), bf16),
            pltpu.VMEM((4, 2, 2, 3, 192, 256), bf16),
            pltpu.VMEM((192, 192), bf16),
            pltpu.VMEM((4, SUF, HD), bf16),
            pltpu.VMEM((4, HD, SUF), bf16),
            pltpu.VMEM((4, HD, SUF), bf16),
            pltpu.VMEM((4, HD, SUF), bf16),
            pltpu.VMEM((16, HD, 128), bf16),
            pltpu.VMEM((4, 2, rows, width), bf16),
            pltpu.VMEM((4, 2, rows, width), bf16),
            pltpu.VMEM((4, rows, width), bf16),
            pltpu.VMEM((4, rows, width), f32),
            pltpu.VMEM((2, 64, width), bf16),
            pltpu.VMEM((4, 64, width), bf16),
            pltpu.VMEM((4, 64, width), bf16),
            pltpu.VMEM((rows, width), bf16),
            pltpu.SemaphoreType.DMA((SEMS,)),
            pltpu.SemaphoreType.DMA((SEMS,)),
            pltpu.SemaphoreType.DMA((16,)),
            pltpu.SemaphoreType.DMA((16,)),
            pltpu.SemaphoreType.DMA((8,)),
        ],
        compiler_params=pltpu.CompilerParams(
            collective_id=0, has_side_effects=True, vmem_limit_bytes=67_043_328
        ),
        name="layer_kernel",
    )(*scalars, *arrays)


def local(
    tokens,
    attention_gain,
    feed_gain,
    w_query,
    w_key,
    w_value,
    w_out,
    w_gate,
    w_up,
    w_down,
    prefix_cache,
    lengths,
    member,
    owners,
):
    prefix_length = prefix_cache.shape[2]
    half = np.arange(HD // 2).astype(np.float32)
    frequency = np.float32(rope_base) ** (-(half * np.float32(2.0) / np.float32(HD)))
    positions = (np.arange(SUF) + prefix_length).astype(np.float32)
    angles = (frequency[:, None] * positions[None, :]).astype(np.float64)
    hidden, cache = layer(
        (lengths, member, owners),
        (
            prefix_cache[:, 0].transpose(0, 2, 1),
            tokens,
            w_query,
            w_key.T,
            w_value.T,
            w_out,
            w_gate,
            w_up,
            w_down.T,
            attention_gain[None, :],
            feed_gain[None, :],
            np.cos(angles).astype(np.float32),
            np.sin(angles).astype(np.float32),
        ),
    )
    return (hidden, cache.transpose(0, 2, 1))


def solution(mesh):
    placed = (
        P(("req", "mdl"), None),
        P(),
        P(),
        P("req", "mdl"),
        P("req", "mdl"),
        P("req", "mdl"),
        P("mdl", "req"),
        P("req", "mdl"),
        P("req", "mdl"),
        P("mdl", "req"),
        P(None, "req", None, "mdl"),
        P(),
        P(),
        P(),
    )
    return jax.shard_map(
        local,
        mesh=mesh,
        in_specs=placed,
        out_specs=(P(("req", "mdl"), None), P(None, "req", "mdl")),
        check_vma=False,
    )
```

```python
import math

import jax
import jax.numpy as jnp
import numpy as np
from jax import lax
from jax.experimental import pallas as pl
from jax.experimental.pallas import tpu as pltpu
from jax.sharding import PartitionSpec as P

HD = 96
HALF = 48
SUF = 512
rope_base = 100000.0
norm_eps = 1e-05
MESH = pl.DeviceIdType.MESH
LOG2E = 1.4426950408889634


def places():
    req = lax.axis_index("req")
    mdl = lax.axis_index("mdl")
    return req, mdl


class Hub:
    def __init__(self, send, recv):
        self.send, self.recv, self.made, self.pending = send, recv, [], []

    def copy(self, src, dst, device, awaited=True):
        index = len(self.made)
        made = pltpu.make_async_remote_copy(
            src_ref=src,
            dst_ref=dst,
            send_sem=self.send.at[index],
            recv_sem=self.recv.at[index],
            device_id=device,
            device_id_type=MESH,
        )
        made.start()
        self.made.append(made)
        if not awaited:
            self.pending.append(made)
        return made

    def shared(self):
        for made in self.pending:
            made.wait_recv()
        self.pending = []

    def finish(self):
        self.shared()
        for made in self.made:
            made.wait_send()


class Ring:
    def __init__(self, hub, region, piece, dev, u):
        self.hub, self.region, self.piece, self.dev = hub, region, piece, dev
        self.here, self.up_to, self.down_to, self.opposite = (
            u, lax.rem(u + 1, 4), lax.rem(u + 3, 4), lax.rem(u + 2, 4)
        )

    def start(self, src=None):
        block = self.region(self.here)
        src = block if src is None else src
        self.up = self.hub.copy(src, block, self.dev(self.up_to))
        self.down = self.hub.copy(src, block, self.dev(self.down_to))

    def near(self):
        self.up.wait_recv()
        self.down.wait_recv()

    def arrive(self, waited=False):
        if not waited:
            self.up.wait_recv()
        low = self.piece(self.down_to, 0)
        self.far_low = self.hub.copy(low, low, self.dev(self.up_to))
        if not waited:
            self.down.wait_recv()
        high = self.piece(self.up_to, 1)
        self.far_high = self.hub.copy(high, high, self.dev(self.down_to))

    def finish(self):
        self.far_low.wait_recv()
        self.far_high.wait_recv()

    def start_split(self, src=None):
        up, down = self.dev(self.up_to), self.dev(self.down_to)
        to = [self.piece(self.here, h) for h in range(2)]
        of = to if src is None else [src.at[h] for h in range(2)]
        self.up = self.hub.copy(of[0], to[0], up)
        self.down = self.hub.copy(of[1], to[1], down)
        self.up_rest = self.hub.copy(of[1], to[1], up)
        self.down_rest = self.hub.copy(of[0], to[0], down)

    def rest(self):
        self.up_rest.wait_recv()
        self.down_rest.wait_recv()

    def share(self, u, device, awaited=True):
        block = self.region(u)
        return self.hub.copy(block, block, device, awaited)


class Direct:
    def __init__(self, hub, region, dev, u):
        self.hub, self.region, self.dev, self.here = hub, region, dev, u

    def start(self, src=None):
        block = self.region(self.here)
        src = block if src is None else src
        self.sent = [
            self.hub.copy(src, block, self.dev(lax.rem(self.here + step, 4)))
            for step in (1, 3, 2)
        ]

    def finish(self):
        for made in self.sent:
            made.wait_recv()


class Spread:
    def __init__(self, hub, own, block, piece, u, v, dev, partner):
        self.hub, self.own, self.partner = hub, own, partner
        self.here, self.other = block(u, v), block(u, 1 - v)
        self.pair_dev = dev(u, 1 - v)
        self.handed = []

        def ring(w):
            return Ring(
                hub,
                lambda p: block(p, w),
                lambda p, h: piece(block(p, w), h),
                lambda p: dev(p, v),
                u,
            )

        self.rings = (ring(v), ring(1 - v))

    def start_pair(self):
        self.pair = self.hub.copy(self.own, self.here, self.pair_dev)

    def start_ring(self):
        self.rings[0].start(self.own)
        self.handed.append(self.hub.copy(self.own, self.here, self.partner))

    def pair_arrived(self):
        self.pair.wait_recv()
        self.rings[1].start()
        self.handed.append(self.hub.copy(self.other, self.other, self.partner))

    def ring_arrived(self, which):
        ring = self.rings[which]
        ring.arrive()
        self.hand(ring, ring.down_to)
        self.hand(ring, ring.up_to)

    def far_arrived(self, which):
        ring = self.rings[which]
        ring.finish()
        self.hand(ring, ring.opposite)

    def hand(self, ring, u):
        block = ring.region(u)
        self.handed.append(self.hub.copy(block, block, self.partner))

    def shared(self):
        for made in self.handed:
            made.wait_recv()


SEMS = 136
KV_EARLY = 3072


def layer_kernel(
    lengths, member, owners,
    kv_in, tok_in, wq_in, wk_in, wv_in, wo_in, wg_in, wu_in, wd_in,
    gain_ref, feed_gain_ref, cos_ref, sin_ref,
    out_ref, cache_ref,
    kv_all, tok_all, wqkv, wo, wm, pack, query, keys, values, att_out, att,
    rows_all, part, from_pair, sums, relay, plain, joined, to_relay,
    send, recv, a2a_send, a2a_recv, local_sem,
):
    req, mdl = places()
    x, yh = req // 2, lax.rem(req, 2)
    z, yl, core = mdl // 4, lax.rem(mdl // 2, 2), lax.rem(mdl, 2)
    y = yh * 2 + yl
    quarter = lax.rem(mdl, 4)
    width = tok_in.shape[1]
    partner = {"req": req, "mdl": z * 4 + yl * 2 + 1 - core}
    rows = pl.ds(pl.multiple_of(core * HALF, HALF), HALF)

    def kv_dev(u, v):
        return {"req": u * 2 + v, "mdl": mdl}

    def tok_dev(u, v):
        return {"req": req, "mdl": u * 4 + v * 2 + core}

    def x_dev(u):
        return kv_dev(u, yh)

    def y_dev(u):
        return {"req": x * 2 + u // 2, "mdl": z * 4 + lax.rem(u, 2) * 2 + core}

    def z_dev(u):
        return tok_dev(u, yl)

    barrier = pltpu.get_barrier_semaphore()
    peers = [kv_dev(x, 1 - yh)]
    peers += [x_dev(lax.rem(x + step, 4)) for step in (1, 2, 3)]
    peers += [y_dev(lax.rem(y + step, 4)) for step in (1, 3)]
    peers += [{"req": req, "mdl": lax.rem(mdl + step, 16)} for step in range(1, 16)]
    for peer in peers:
        pl.semaphore_signal(barrier, inc=1, device_id=peer, device_id_type=MESH)

    keep = []

    def store(src, dst):
        made = pltpu.make_async_copy(src, dst, local_sem.at[len(keep)])
        made.start()
        keep.append(made)

    store(wo_in, wo.at[z, core, x, yh, yl])
    for kind, ref in enumerate((wg_in, wu_in, wd_in)):
        store(ref, wm.at[x, yh, yl, kind])
    store(kv_in, kv_all.at[req, :, rows, :])
    store(tok_in, tok_all.at[mdl])
    pack[:, 0:HD] = wq_in[...]
    pack[:, HD : HD + HALF] = jnp.transpose(wk_in[...])
    pack[:, HD + HALF : 2 * HD] = jnp.transpose(wv_in[...])
    pl.semaphore_wait(barrier, len(peers))

    hub = Hub(send, recv)
    early, late = pl.ds(0, KV_EARLY), pl.ds(KV_EARLY, kv_all.shape[3] - KV_EARLY)
    kv_ring = Ring(
        hub,
        lambda u: kv_all.at[u * 2 + yh, :, rows],
        lambda u, h: kv_all.at[u * 2 + yh, h, rows],
        x_dev, x,
    )
    kv_other = Ring(
        hub,
        lambda u: kv_all.at[u * 2 + 1 - yh, :, rows, early],
        lambda u, h: kv_all.at[u * 2 + 1 - yh, h, rows, early],
        x_dev, x,
    )
    kv_pair = kv_dev(x, 1 - yh)
    handed = []

    def hand(block):
        handed.append(hub.copy(block, block, partner))

    def cross(u):
        block = kv_all.at[u * 2 + yh, :, rows, late]
        return hub.copy(block, block, kv_pair)

    def crossed(u, made):
        made.wait_recv()
        hand(kv_all.at[u * 2 + 1 - yh, :, rows, late])

    tok = Spread(
        hub, tok_in,
        lambda u, v: tok_all.at[u * 4 + v * 2 + core],
        lambda ref, h: ref.at[pl.ds(64 * h, 64)],
        z, yl, tok_dev, partner,
    )
    qkv = Spread(
        hub, pack,
        lambda u, v: wqkv.at[u * 2 + v, core],
        lambda ref, h: ref.at[pl.ds(96 * h, 96)],
        x, yh, kv_dev, partner,
    )
    wo_x = Direct(hub, lambda u: wo.at[z, core, u, yh, yl], x_dev, x)
    wo_y = Direct(hub, lambda u: wo.at[z, core, :, u // 2, lax.rem(u, 2)], y_dev, y)
    wo_z = Ring(
        hub,
        lambda u: wo.at[u, core],
        lambda u, h: wo.at[u, core, pl.ds(2 * h, 2)],
        z_dev, z,
    )
    wm_x = Ring(
        hub,
        lambda u: wm.at[u, yh, yl],
        lambda u, h: wm.at[u, yh, yl, :, pl.ds(96 * h, 96)],
        x_dev, x,
    )

    def wm_ring(step):
        u_x = lax.rem(x + step, 4)
        return Ring(
            hub,
            lambda u: wm.at[u_x, u // 2, lax.rem(u, 2)],
            lambda u, h: wm.at[u_x, u // 2, lax.rem(u, 2), :, pl.ds(96 * h, 96)],
            y_dev, y,
        )

    wm_y = [wm_ring(step) for step in range(4)]

    def project(r, carry):
        numbers = tok_all[pl.ds(4 * r, 4)].reshape(SUF, width).astype(jnp.float32)
        scale = lax.rsqrt(jnp.mean(numbers * numbers, axis=-1, keepdims=True) + norm_eps)
        normed = (numbers * scale * gain_ref[...].astype(jnp.float32)).astype(jnp.bfloat16)
        halves = [
            jnp.transpose(
                jnp.dot(
                    normed, wqkv[:, c].reshape(width, 192), preferred_element_type=jnp.float32
                )
            )
            for c in range(2)
        ]
        cosine, sine = cos_ref[...], sin_ref[...]

        def rotate(block):
            low, high = block[:HALF], block[HALF:]
            return jnp.concatenate(
                [low * cosine - high * sine, high * cosine + low * sine], axis=0
            )

        first = core == 0
        query_raw = jnp.where(first, halves[0][:HD], halves[1][:HD])
        keys_wide = rotate(jnp.concatenate([half[HD : HD + HALF] for half in halves], axis=0))
        values_wide = jnp.concatenate([half[HD + HALF :] for half in halves], axis=0)
        query[r] = jnp.transpose(rotate(query_raw)).astype(jnp.bfloat16)
        keys[r] = keys_wide.astype(jnp.bfloat16)
        values[r] = values_wide.astype(jnp.bfloat16)
        length = lengths[req * 4 + r]
        live = (lax.broadcasted_iota(jnp.int32, (HALF, SUF), 1) < length).astype(jnp.float32)
        columns = pl.ds(pl.multiple_of(r * SUF, SUF), SUF)
        for kind, wide in enumerate((keys_wide, values_wide)):
            own = jnp.where(first, wide[:HALF], wide[HALF:])
            cache_ref[kind, :, columns] = (own * live).astype(jnp.bfloat16)
        return carry

    def attend(i, carry):
        r = lax.rem(z + 1 + i, 4)
        length = lengths[req * 4 + r]
        slot = owners[member[req * 4 + r]]
        factor = LOG2E / math.sqrt(HD)
        chunk = 1024
        top = total = summed = None
        for j in range(0, kv_all.shape[3] + 1, chunk):
            own = j == kv_all.shape[3]
            if own:
                key_part, value_part = keys[r], values[r]
            else:
                key_part = kv_all[slot, 0, :, j : j + chunk]
                value_part = kv_all[slot, 1, :, j : j + chunk]
            scores = jnp.dot(query[r], key_part, preferred_element_type=jnp.float32)
            if own:
                row = lax.broadcasted_iota(jnp.int32, scores.shape, 0)
                column = lax.broadcasted_iota(jnp.int32, scores.shape, 1)
                allowed = (column <= row) & (column < length)
                scores = jnp.where(allowed, scores, -1e30)
            part_top = jnp.max(scores, axis=-1, keepdims=True)
            new_top = part_top if top is None else jnp.maximum(top, part_top)
            weights = jnp.exp2((scores - new_top) * factor)
            if own:
                weights = jnp.where(allowed, weights, 0.0)
            part_total = jnp.sum(weights, axis=-1, keepdims=True)
            part_sum = lax.dot_general(
                weights.astype(jnp.bfloat16),
                value_part,
                (((1,), (1,)), ((), ())),
                preferred_element_type=jnp.float32,
            )
            if top is None:
                total, summed = part_total, part_sum
            else:
                carried = jnp.exp2((top - new_top) * factor)
                total = total * carried + part_total
                summed = summed * carried + part_sum
            top = new_top
        att_out[r] = jnp.transpose(summed / total).astype(jnp.bfloat16)
        for j in range(4):

            @pl.when(r * 4 + j != mdl)
            def _():
                pltpu.make_async_remote_copy(
                    src_ref=att_out.at[r, :, pl.ds(128 * j, 128)],
                    dst_ref=att.at[mdl],
                    send_sem=a2a_send.at[i * 4 + j],
                    recv_sem=a2a_recv.at[i * 4 + quarter],
                    device_id={"req": req, "mdl": r * 4 + j},
                    device_id_type=MESH,
                ).start()

        return carry

    kv_here = kv_ring.region(x)
    wo_x.start(wo_in)
    tok.start_pair()
    kv_ring.start_split(kv_in)
    tok.start_ring()
    qkv.start_pair()
    kv_over = hub.copy(kv_in, kv_here, kv_pair)
    qkv.start_ring()
    handed.append(hub.copy(kv_in, kv_here, partner))
    store(pack, wqkv.at[req, core])
    keep[0].wait()
    wo_x.finish()
    wo_y.start()
    kv_ring.arrive()
    tok.pair_arrived()
    tok.ring_arrived(0)
    qkv.pair_arrived()
    for made in keep[1:4]:
        made.wait()
    wm_x.start()
    kv_ring.rest()
    cross_low = cross(kv_ring.down_to)
    cross_high = cross(kv_ring.up_to)
    hand(kv_ring.region(kv_ring.down_to))
    hand(kv_ring.region(kv_ring.up_to))
    qkv.ring_arrived(0)
    kv_over.wait_recv()
    kv_other.start_split()
    hand(kv_all.at[x * 2 + 1 - yh, :, rows])
    tok.ring_arrived(1)
    qkv.ring_arrived(1)
    kv_ring.finish()
    cross_far = cross(kv_ring.opposite)
    hand(kv_ring.region(kv_ring.opposite))
    wm_y[0].start()
    wo_y.finish()
    wo_z.start()
    wo_z.share(z, partner, False)
    wm_x.near()
    wm_y[3].start()
    wm_y[1].start()
    tok.far_arrived(0)
    tok.far_arrived(1)
    qkv.far_arrived(0)
    kv_other.arrive()
    wm_x.arrive(True)
    qkv.far_arrived(1)
    for made in keep[4:]:
        made.wait()
    tok.shared()
    qkv.shared()
    lax.fori_loop(0, 4, project, 0)
    crossed(kv_ring.down_to, cross_low)
    crossed(kv_ring.up_to, cross_high)
    kv_other.rest()
    hand(kv_other.region(kv_other.down_to))
    hand(kv_other.region(kv_other.up_to))
    crossed(kv_ring.opposite, cross_far)
    kv_other.finish()
    hand(kv_other.region(kv_other.opposite))
    for made in handed:
        made.wait_recv()
    wm_y[0].arrive()
    wo_z.arrive()
    wo_z.share(wo_z.down_to, partner, False)
    wo_z.share(wo_z.up_to, partner, False)
    attend(0, 0)
    wm_x.finish()
    wm_y[2].start()
    attend(1, 0)
    wo_z.finish()
    wo_z.share(wo_z.opposite, partner, False)
    wm_y[3].arrive()
    wm_y[1].arrive()
    attend(2, 0)
    attend(3, 0)
    wm_y[2].arrive()
    att[mdl] = att_out[z, :, pl.ds(pl.multiple_of(quarter * 128, 128), 128)]

    def exchange(i, j, sending):
        k = i * 4 + j
        made = pltpu.make_async_remote_copy(
            src_ref=att_out.at[0, :, pl.ds(0, 128)],
            dst_ref=att.at[j],
            send_sem=a2a_send.at[k],
            recv_sem=a2a_recv.at[k],
            device_id=partner,
            device_id_type=MESH,
        )

        def wait():
            made.wait_send() if sending else made.wait_recv()

        if i < 3:
            wait()
        else:
            pl.when(quarter != j)(wait)

    hub.shared()
    for i in range(4):
        for j in range(4):
            exchange(i, j, False)
    attended = jnp.transpose(att[...].reshape(16 * HD, 128))
    own_rows = rows_all.at[z, core]
    for u in range(4):
        attention = jnp.concatenate(
            [
                jnp.dot(
                    attended,
                    jnp.concatenate(
                        [wo[k // 4, k % 2, u, v, (k // 2) % 2] for k in range(16)], axis=0
                    ),
                    preferred_element_type=jnp.float32,
                )
                for v in range(2)
            ],
            axis=1,
        )
        here = slice(384 * u, 384 * u + 384)
        own_rows[:, here] = (tok_all[mdl, :, here].astype(jnp.float32) + attention).astype(jnp.bfloat16)

    def peer(du, flip=False):
        other = 1 - core if flip else core
        return {"req": req, "mdl": lax.rem(z + du, 4) * 4 + yl * 2 + other}

    go = hub.copy
    gathered = Ring(
        hub,
        lambda u: rows_all.at[u, core],
        lambda u, h: rows_all.at[u, core, pl.ds(64 * h, 64)],
        z_dev, z,
    )
    gathered.start_split()
    across = go(own_rows, own_rows, partner)
    for ring in wm_y:
        ring.finish()

    def feed(slot, du):
        there = rows_all.at[lax.rem(z + du, 4)]
        numbers = there[...].reshape(256, width).astype(jnp.float32)
        scale = lax.rsqrt(jnp.mean(numbers * numbers, axis=-1, keepdims=True) + norm_eps)
        normed = (numbers * scale * feed_gain_ref[...].astype(jnp.float32)).astype(jnp.bfloat16)
        active = []
        for block in range(2):
            gate = jnp.dot(
                normed,
                wm[:, :, block, 0].reshape(width, 256),
                preferred_element_type=jnp.float32,
            )
            lift = jnp.dot(
                normed,
                wm[:, :, block, 1].reshape(width, 256),
                preferred_element_type=jnp.float32,
            )
            active.append((gate / (1.0 + jnp.exp(-gate)) * lift).astype(jnp.bfloat16))
        copies = []
        for u in range(4):
            parts = [
                lax.dot_general(
                    active[block],
                    wm[u, :, block, 2].reshape(384, 256),
                    (((1,), (1,)), ((), ())),
                    preferred_element_type=jnp.float32,
                )
                for block in range(2)
            ]
            part[slot, :, :, 384 * u : 384 * u + 384] = (
                (parts[0] + parts[1]).astype(jnp.bfloat16).reshape(2, 128, 384)
            )
            if u % 2:
                side = pl.ds(384 * (u - 1), 768)
                copies.append(
                    go(part.at[slot, 1 - core, :, side], from_pair.at[slot, :, side], partner)
                )
        return copies

    sides = [slice(768 * k, 768 * k + 768) for k in range(2)]

    def pair_sum(slot, copies, which=(0, 1)):
        for k in which:
            copies[k].wait_recv()
            side = sides[k]
            sums[slot, :, side] = part[slot, core, :, side].astype(jnp.float32) + from_pair[
                slot, :, side
            ].astype(jnp.float32)

    across.wait_recv()
    pair0 = feed(0, 0)
    gathered.arrive()
    gathered.up_rest.wait_recv()
    low_p = gathered.share(gathered.down_to, partner)
    gathered.down_rest.wait_recv()
    high_p = gathered.share(gathered.up_to, partner)
    low_p.wait_recv()
    pair3 = feed(3, 3)
    gathered.finish()
    far_p = gathered.share(gathered.opposite, partner)
    high_p.wait_recv()
    pair1 = feed(1, 1)
    pair_sum(3, pair3)
    plain[0] = sums[3, 0:64].astype(jnp.bfloat16)
    plain_a = go(plain.at[0], plain.at[2], peer(3))
    far_p.wait_recv()
    pair2 = feed(2, 2)
    pair_sum(1, pair1)
    plain[1] = sums[1, 64:128].astype(jnp.bfloat16)
    plain_b = go(plain.at[1], plain.at[3], peer(1))
    relays = []
    for k, side in enumerate(sides):
        pair_sum(2, pair2, (k,))
        to_relay[:, side] = sums[2, :, side].astype(jnp.bfloat16)
        cols = pl.ds(768 * k, 768)
        relays.append(
            (
                go(to_relay.at[pl.ds(0, 64), cols], relay.at[0, :, cols], peer(1)),
                go(to_relay.at[pl.ds(64, 64), cols], relay.at[1, :, cols], peer(3)),
            )
        )
    pair_sum(0, pair0)
    joins = []
    for k, side in enumerate(sides):
        cols = pl.ds(768 * k, 768)
        for h, (slot, du) in enumerate(((1, 1), (3, 3))):
            relays[k][h].wait_recv()
            joined[h, :, side] = (
                sums[slot, 64 * h : 64 * h + 64, side] + relay[h, :, side].astype(jnp.float32)
            ).astype(jnp.bfloat16)
            joins.append(go(joined.at[h, :, cols], joined.at[2 + h, :, cols], peer(du)))
    plain_a.wait_recv()
    plain_b.wait_recv()
    for copy in joins:
        copy.wait_recv()
    for h in range(2):
        here = slice(64 * h, 64 * h + 64)
        feed_sum = (
            sums[0, here]
            + plain[2 + h].astype(jnp.float32)
            + joined[2 + h].astype(jnp.float32)
        )
        place = quarter * 128 + 64 * h + lax.broadcasted_iota(jnp.int32, (64, 1), 0)
        live = (place < lengths[req * 4 + z]).astype(jnp.float32)
        out_ref[here, :] = (
            (own_rows[here, :].astype(jnp.float32) + feed_sum) * live
        ).astype(jnp.bfloat16)
    for i in range(4):
        for j in range(4):
            exchange(i, j, True)
    hub.finish()


def layer(scalars, arrays):
    kv_own, tokens = arrays[:2]
    rows, width = tokens.shape
    bf16, f32 = jnp.bfloat16, jnp.float32
    vmem = pl.BlockSpec(memory_space=pltpu.VMEM)
    hbm = pl.BlockSpec(memory_space=pl.ANY)
    return pl.pallas_call(
        layer_kernel,
        out_shape=(
            jax.ShapeDtypeStruct((rows, width), bf16),
            jax.ShapeDtypeStruct((2, HALF, 4 * SUF), bf16),
        ),
        in_specs=[pl.BlockSpec(memory_space=pltpu.SMEM)] * len(scalars)
        + [hbm, hbm, vmem, vmem, vmem, hbm, hbm, hbm, hbm, vmem, vmem, vmem, vmem],
        out_specs=[vmem] * 2,
        scratch_shapes=[
            pltpu.VMEM((8, 2, HD, kv_own.shape[2]), bf16),
            pltpu.VMEM((16, rows, width), bf16),
            pltpu.VMEM((8, 2, 192, 192), bf16),
            pltpu.VMEM((4, 2, 4, 2, 2, HD, 192), bf16),
            pltpu.VMEM((4, 2, 2, 3, 192, 256), bf16),
            pltpu.VMEM((192, 192), bf16),
            pltpu.VMEM((4, SUF, HD), bf16),
            pltpu.VMEM((4, HD, SUF), bf16),
            pltpu.VMEM((4, HD, SUF), bf16),
            pltpu.VMEM((4, HD, SUF), bf16),
            pltpu.VMEM((16, HD, 128), bf16),
            pltpu.VMEM((4, 2, rows, width), bf16),
            pltpu.VMEM((4, 2, rows, width), bf16),
            pltpu.VMEM((4, rows, width), bf16),
            pltpu.VMEM((4, rows, width), f32),
            pltpu.VMEM((2, 64, width), bf16),
            pltpu.VMEM((4, 64, width), bf16),
            pltpu.VMEM((4, 64, width), bf16),
            pltpu.VMEM((rows, width), bf16),
            pltpu.SemaphoreType.DMA((SEMS,)),
            pltpu.SemaphoreType.DMA((SEMS,)),
            pltpu.SemaphoreType.DMA((16,)),
            pltpu.SemaphoreType.DMA((16,)),
            pltpu.SemaphoreType.DMA((8,)),
        ],
        compiler_params=pltpu.CompilerParams(
            collective_id=0, has_side_effects=True, vmem_limit_bytes=67_043_328
        ),
        name="layer_kernel",
    )(*scalars, *arrays)


def local(
    tokens,
    attention_gain,
    feed_gain,
    w_query,
    w_key,
    w_value,
    w_out,
    w_gate,
    w_up,
    w_down,
    prefix_cache,
    lengths,
    member,
    owners,
):
    prefix_length = prefix_cache.shape[2]
    half = np.arange(HD // 2).astype(np.float32)
    frequency = np.float32(rope_base) ** (-(half * np.float32(2.0) / np.float32(HD)))
    positions = (np.arange(SUF) + prefix_length).astype(np.float32)
    angles = (frequency[:, None] * positions[None, :]).astype(np.float64)
    hidden, cache = layer(
        (lengths, member, owners),
        (
            prefix_cache[:, 0].transpose(0, 2, 1),
            tokens,
            w_query,
            w_key.T,
            w_value.T,
            w_out,
            w_gate,
            w_up,
            w_down.T,
            attention_gain[None, :],
            feed_gain[None, :],
            np.cos(angles).astype(np.float32),
            np.sin(angles).astype(np.float32),
        ),
    )
    return (hidden, cache.transpose(0, 2, 1))


def solution(mesh):
    placed = (
        P(("req", "mdl"), None),
        P(),
        P(),
        P("req", "mdl"),
        P("req", "mdl"),
        P("req", "mdl"),
        P("mdl", "req"),
        P("req", "mdl"),
        P("req", "mdl"),
        P("mdl", "req"),
        P(None, "req", None, "mdl"),
        P(),
        P(),
        P(),
    )
    return jax.shard_map(
        local,
        mesh=mesh,
        in_specs=placed,
        out_specs=(P(("req", "mdl"), None), P(None, "req", "mdl")),
        check_vma=False,
    )
```
